32 devices in a mesh: group: 2 (over y), row: 4 (over x, core), col: 4 (over z).
Axes of the slice: x: 2, y: 2, z: 4, core: 2. Of those that a mesh axis runs over, the one named last changes fastest.
Arguments:
- patches: bfloat16 [64, 64, 1280], P(('group', 'row'), 'col'), parts along dimension 0, may hold values from -6 to 6
- patch_gain: bfloat16 [1280], replicated, may hold values from 0.25 to 1.75
- patch_bias: bfloat16 [1280], replicated, may hold values from -3 to 3
- merger_up: bfloat16 [5120, 5120], P('col', 'row'), may hold values from -0.078125 to 0.078125
- merger_up_bias: bfloat16 [5120], P('row'), may hold values from -3 to 3
- merger_down: bfloat16 [5120, 8192], P('row', 'col')
- merger_down_bias: bfloat16 [8192], P('col'), may hold values from -1.796875 to 1.796875
- norm_gain: bfloat16 [8192], P('col'), may hold values from 0.25 to 1.75
- w_gate: bfloat16 [8192, 14784], P('col', 'row'), may hold values from -0.0625 to 0.0625
- w_up: bfloat16 [8192, 14784], P('col', 'row'), may hold values from -0.0625 to 0.0625
- hidden_cotangent: bfloat16 [1024, 14784], P(('group', 'col'), 'row'), parts along dimension 0, may hold values from -0.59765625 to 0.59765625
- placement: int32 [64], P('group'), parts along dimension 0, may hold values from 0 to 31, as said below
- patch_counts: int32 [64], P('group'), parts along dimension 0, may hold values from 4 to 64, as said below
Outputs:
- merger_up_grad: float32 [10240, 5120], P(('group', 'col'), 'row'), parts along dimension 0
- merger_up_bias_grad: float32 [10240], P(('group', 'row')), parts along dimension 0
- merger_down_grad: float32 [10240, 8192], P(('group', 'row'), 'col'), parts along dimension 0
- merger_down_bias_grad: float32 [16384], P(('group', 'col')), parts along dimension 0
The draws below stay inside these ranges and needn't reach their ends.
There are 2 independent parts, one for each index of `group`. The reference program is written for one: setup_inputs(seed, part) draws one part's arguments, and reference() takes and returns one part's arrays. A program takes and returns all parts, laid end to end along the dimension named above; an argument that names none is the same for every part. Nothing has to cross between parts.
Inputs may be any that keep to these rules, and one draw needn't show every extreme that they name: `placement`: A permutation of the images onto the sequence blocks. Block b lies on index b // 8 of row, and image i on index i // 8. The 8 images of one index of row fill at most 2 blocks of any one index of row, and exactly 2 for some pair of indices in every draw. Every count is a multiple of 4; image i's first patch_counts[i] // 4 merged slots are real and the others are padding; some image has exactly 64 patches in every draw.
All inputs are finite; a program needn't handle non-finite values.
Results may differ from the reference program's by a relative error of at most 0.034.
Values may be sent and summed in bfloat16 or wider, within the bound.
A program may use at most 192 MiB of HBM per device.

```python
import math
import jax
import jax.numpy as jnp
from jax import lax

D = 8192
PATCH_DIM = 1280
MH = 5120
FFW = 14784
BLK = 16
IMG_ROW = 8
PATCHES = 64
MDIM = 5120
IMAGES = 32
TOKENS = 512
N_ROW = 4
N_COL = 4


def draw_merger_down(key, part):
    key_base, key_scale = jax.random.split(key)
    base = jax.random.normal(key_base, (MH, D), jnp.float32)
    rise = math.log(20.0)
    column = jnp.arange(D, dtype=jnp.float32) / D
    jitter = jax.random.uniform(key_scale, (D,), jnp.float32, -0.5, 0.5)
    scale = jnp.exp(rise * (column - 0.5) + math.log(2.0) * jitter)
    return (base * (scale / math.sqrt(MH))[None, :]).astype(jnp.bfloat16)


def draw_placement(key, part):
    groups = IMAGES // IMG_ROW
    key_order, key_rest, key_turn, key_slot = jax.random.split(jax.random.fold_in(key, 11), 4)
    order = jax.random.permutation(key_order, groups)
    remaining = jax.random.permutation(key_rest, jnp.concatenate([order[1:], order[1:]]))
    shifts = jnp.concatenate([order[:1], order[:1], remaining[:IMG_ROW - 2]])
    turns = jax.vmap(lambda one_key: jax.random.permutation(one_key, IMG_ROW))(jax.random.split(key_turn, groups))
    slots = jax.vmap(lambda one_key: jax.random.permutation(one_key, IMG_ROW))(jax.random.split(key_slot, groups))
    image_ids = jnp.arange(IMAGES, dtype=jnp.int32)
    source = image_ids // IMG_ROW
    local = image_ids % IMG_ROW
    which = turns[source, local]
    target = (source + shifts[which]) % groups
    return (target * IMG_ROW + slots[target, which]).astype(jnp.int32)


def draw_patch_counts(key, part):
    key_count, key_full = jax.random.split(jax.random.fold_in(key, 23))
    merged = jax.random.randint(key_count, (IMAGES,), 1, BLK + 1)
    chosen = jax.random.randint(key_full, (), 0, IMAGES)
    merged = jnp.where(jnp.arange(IMAGES) == chosen, BLK, merged)
    return (4 * merged).astype(jnp.int32)


def steps_of(rng, extent, cuts, least, high):
    def one(dim, shards_of):
        draws = jax.random.uniform(jax.random.fold_in(jax.random.fold_in(rng, 6), dim), (shards_of,), jnp.float32, least / len(cuts), high / len(cuts))
        return jnp.repeat(jnp.exp(draws), extent[dim] // shards_of).reshape((-1,) + (1,) * (len(extent) - dim - 1))

    loudness = one(*cuts[0])
    for cut in cuts[1:]:
        loudness = loudness * one(*cut)
    return loudness


def normal_values(rng, dims, scale, reach, cuts=(), held_as=jnp.bfloat16):
    result = scale * jax.random.normal(rng, dims, jnp.float32)
    if cuts:
        result = result * steps_of(rng, dims, cuts, -0.22, 0.18)
    return jnp.clip(result, -reach, reach).astype(held_as)


def setup_inputs(seed: int = 0, part: int = 0) -> dict:
    key_list = jax.random.split(jax.random.key(seed), 14)
    part_splits = jax.random.split(jax.random.fold_in(key_list[13], part), 14)
    return {
        "patches": normal_values(part_splits[0], (IMAGES, PATCHES, PATCH_DIM), 1.0, 6.0, ((0, 4), (1, 4))),
        "patch_gain": jnp.clip(1.0 + 0.15 * jax.random.normal(key_list[1], (PATCH_DIM,), jnp.float32), 0.25, 1.75).astype(jnp.bfloat16),
        "patch_bias": normal_values(key_list[2], (PATCH_DIM,), 0.5, 3.0),
        "merger_up": normal_values(key_list[3], (MDIM, MH), MDIM ** -0.5, 0.078125, ((0, 4), (1, 4))),
        "merger_up_bias": normal_values(key_list[4], (MH,), 0.5, 3.0, ((0, 4),)),
        "merger_down": draw_merger_down(jax.random.fold_in(key_list[13], 71), part),
        "merger_down_bias": normal_values(key_list[6], (D,), 0.3, 1.796875, ((0, 4),)),
        "norm_gain": jnp.clip(1.0 + 0.15 * jax.random.normal(key_list[7], (D,), jnp.float32), 0.25, 1.75).astype(jnp.bfloat16),
        "w_gate": normal_values(key_list[8], (D, FFW), D ** -0.5, 0.0625, ((0, 4), (1, 4))),
        "w_up": normal_values(key_list[9], (D, FFW), D ** -0.5, 0.0625, ((0, 4), (1, 4))),
        "hidden_cotangent": normal_values(part_splits[10], (TOKENS, FFW), 0.1, 0.59765625, ((0, 4), (1, 4))),
        "placement": draw_placement(jax.random.fold_in(jax.random.fold_in(key_list[13], part), 71), part),
        "patch_counts": draw_patch_counts(jax.random.fold_in(jax.random.fold_in(key_list[13], part), 71), part),
    }


EPS_PATCH = 1e-06
EPS_NORM = 1e-06

def rounded(inputs):
    return lax.optimization_barrier(inputs.astype(jnp.bfloat16)).astype(jnp.float32)

def gelu_slope(inputs):
    cumulative = 0.5 * (1.0 + jax.scipy.special.erf(inputs / math.sqrt(2.0)))
    return cumulative + inputs * jnp.exp(-0.5 * inputs * inputs) / math.sqrt(2.0 * math.pi)

def blocked_product(factors, pieces):
    row_count = factors[0][0].shape[0]
    col_count = factors[0][1].shape[1]
    block_width = factors[0][0].shape[1] // pieces

    def step(running, block_index):
        offset = block_index * block_width
        block_term = jnp.zeros((row_count, col_count), jnp.float32)
        for left_side, right_side in factors:
            left_block = lax.dynamic_slice_in_dim(left_side, offset, block_width, 1)
            right_block = lax.dynamic_slice_in_dim(right_side, offset, block_width, 0)
            block_term = block_term + jnp.dot(left_block, right_block, preferred_element_type=jnp.float32)
        return (running + rounded(block_term), None)
    running, unused = lax.scan(step, jnp.zeros((row_count, col_count), jnp.float32), jnp.arange(pieces, dtype=jnp.int32))
    return running

def reference(patches, patch_gain, patch_bias, merger_up, merger_up_bias, merger_down, merger_down_bias, norm_gain, w_gate, w_up, hidden_cotangent, placement, patch_counts):
    values = patches.astype(jnp.float32)
    center = values - lax.optimization_barrier(jnp.mean(values, axis=-1, keepdims=True))
    spread = lax.optimization_barrier(jnp.mean(center * center, axis=-1, keepdims=True))
    normed_patches = (center * lax.rsqrt(spread + EPS_PATCH) * patch_gain.astype(jnp.float32) + patch_bias.astype(jnp.float32)).astype(jnp.bfloat16)
    image_tokens = normed_patches.reshape(IMAGES, BLK, MDIM)
    image_ids = jnp.arange(IMAGES, dtype=jnp.int32)
    hit_table = placement[:, None] == image_ids[None, :]
    source = lax.optimization_barrier(jnp.sum(jnp.where(hit_table, image_ids[:, None], 0), axis=0)).astype(jnp.int32)
    sequence = image_tokens[source].reshape(TOKENS, MDIM)
    block_fill = lax.optimization_barrier(jnp.sum(jnp.where(hit_table, (patch_counts // 4)[:, None], 0), axis=0)).astype(jnp.int32)
    position = jnp.arange(TOKENS, dtype=jnp.int32)
    valid_rows = position % BLK < block_fill[position // BLK]
    pre_act = blocked_product([(sequence, merger_up)], N_COL) + merger_up_bias.astype(jnp.float32)
    hidden_merge = jax.nn.gelu(pre_act, approximate=False).astype(jnp.bfloat16)
    merged_out = lax.optimization_barrier((blocked_product([(hidden_merge, merger_down)], N_ROW) + merger_down_bias.astype(jnp.float32)).astype(jnp.bfloat16))
    merged_f = merged_out.astype(jnp.float32)
    inv_rms = lax.rsqrt(lax.optimization_barrier(jnp.sum(merged_f * merged_f, axis=1)) / D + EPS_NORM)
    gain = norm_gain.astype(jnp.float32)
    normed = (merged_f * inv_rms[:, None] * gain).astype(jnp.bfloat16)
    gate_out = lax.optimization_barrier(blocked_product([(normed, w_gate)], N_COL).astype(jnp.bfloat16))
    up_out = lax.optimization_barrier(blocked_product([(normed, w_up)], N_COL).astype(jnp.bfloat16))
    gate_f = gate_out.astype(jnp.float32)
    up_f = up_out.astype(jnp.float32)
    cotangent = jnp.where(valid_rows[:, None], hidden_cotangent.astype(jnp.float32), 0.0)
    logistic = jax.nn.sigmoid(gate_f)
    grad_gate = (cotangent * up_f * logistic * (1.0 + gate_f * (1.0 - logistic))).astype(jnp.bfloat16)
    grad_up = (cotangent * gate_f * logistic).astype(jnp.bfloat16)
    grad_normed = blocked_product([(grad_gate, w_gate.T), (grad_up, w_up.T)], N_ROW)
    gained = gain * grad_normed
    inner = lax.optimization_barrier(jnp.sum(merged_f * gained, axis=1))
    grad_merged = lax.optimization_barrier((inv_rms[:, None] * gained - merged_f * (inv_rms * inv_rms * inv_rms / D * inner)[:, None]).astype(jnp.bfloat16))
    merger_down_grad = jnp.dot(hidden_merge.T, grad_merged, preferred_element_type=jnp.float32)
    merger_down_bias_grad = lax.optimization_barrier(jnp.sum(grad_merged.astype(jnp.float32), axis=0))
    grad_hidden = blocked_product([(grad_merged, merger_down.T)], N_COL)
    grad_pre = lax.optimization_barrier((grad_hidden * gelu_slope(pre_act)).astype(jnp.bfloat16))
    merger_up_grad = jnp.dot(sequence.T, grad_pre, preferred_element_type=jnp.float32)
    merger_up_bias_grad = lax.optimization_barrier(jnp.sum(grad_pre.astype(jnp.float32), axis=0))
    return (merger_up_grad, merger_up_bias_grad, merger_down_grad, merger_down_bias_grad)
```

```python
import functools
import math

import jax
import jax.numpy as jnp
from jax import lax
from jax.experimental import pallas as pl
from jax.experimental.pallas import tpu as pltpu
from jax.sharding import PartitionSpec as P

D = 8192
BLK = 16
IMG_ROW = 8


EPS_PATCH = 1e-06
EPS_NORM = 1e-06
CONTRACT_ROWS = (((0,), (0,)), ((), ()))
CONTRACT_COLS = (((1,), (1,)), ((), ()))


def gelu_slope(inputs):
    cumulative = 0.5 * (1.0 + jax.scipy.special.erf(inputs / math.sqrt(2.0)))
    return cumulative + inputs * jnp.exp(-0.5 * inputs * inputs) / math.sqrt(2.0 * math.pi)


def patch_tokens(patches, patch_gain, patch_bias):
    values = patches.astype(jnp.float32)
    center = values - jnp.mean(values, axis=-1, keepdims=True)
    spread = jnp.mean(center * center, axis=-1, keepdims=True)
    normed = center * lax.rsqrt(spread + EPS_PATCH) * patch_gain.astype(
        jnp.float32
    ) + patch_bias.astype(jnp.float32)
    image_count, patch_slots, patch_width = patches.shape
    return normed.astype(jnp.bfloat16).reshape(image_count, patch_slots // 4, 4 * patch_width)


def swiglu_grads(gate_out, up_out, cotangent):
    gate_f = gate_out.astype(jnp.float32)
    up_f = up_out.astype(jnp.float32)
    masked = cotangent.astype(jnp.float32)
    logistic = jax.nn.sigmoid(gate_f)
    grad_gate = (masked * up_f * logistic * (1.0 + gate_f * (1.0 - logistic))).astype(jnp.bfloat16)
    grad_up = (masked * gate_f * logistic).astype(jnp.bfloat16)
    return (grad_gate, grad_up)


def pack_plan(placement, patch_counts, tokens, n_row, n_col, cap):
    images = placement.shape[0]
    rows = tokens // n_col
    blocks = rows // BLK
    ids = jnp.arange(images, dtype=jnp.int32)
    cols = jnp.arange(n_col, dtype=jnp.int32)
    hit = placement[:, None] == ids[None, :]
    fill = jnp.sum(jnp.where(hit, (patch_counts // 4)[:, None], 0), axis=0)
    owner = ids // blocks
    before = (owner[:, None] == owner[None, :]) & (ids[None, :] < ids[:, None])
    start = jnp.sum(jnp.where(before, fill[None, :], 0), axis=1)
    count = jnp.sum(jnp.where(owner[None, :] == cols[:, None], fill[None, :], 0), axis=1)
    over = jnp.maximum(count - cap, 0)
    free = jnp.maximum(cap - count, 0)
    lower = cols[None, :] < cols[:, None]
    over_start = jnp.sum(jnp.where(lower, over[None, :], 0), axis=1)
    free_start = jnp.sum(jnp.where(lower, free[None, :], 0), axis=1)

    def spill_slot(number):
        inside = (number[..., None] >= free_start) & (number[..., None] < free_start + free)
        return jnp.sum(
            jnp.where(inside, cols * cap + count + number[..., None] - free_start, 0), axis=-1
        )

    place = jnp.arange(BLK, dtype=jnp.int32)
    rank = start[:, None] + place[None, :]
    real = place[None, :] < fill[:, None]
    owner_over = jnp.sum(jnp.where(owner[:, None] == cols[None, :], over_start[None, :], 0), axis=1)
    slot = jnp.where(
        rank < cap,
        owner[:, None] * cap + rank,
        spill_slot(owner_over[:, None] + rank - cap),
    )
    slot = jnp.where(real, slot, -1)
    rank = jnp.where(real, rank, -1)
    by_image = jnp.sum(jnp.where(hit[:, :, None], slot[None, :, :], 0), axis=1)
    extra = jnp.arange(rows - cap, dtype=jnp.int32)
    extra_slot = jnp.where(
        extra[None, :] < over[:, None], spill_slot(over_start[:, None] + extra[None, :]), -1
    )
    return slot.reshape(-1), rank.reshape(-1), by_image, extra_slot.reshape(-1)


def one_hot(slots, first, size):
    return (slots[None, :] - first == jnp.arange(size, dtype=jnp.int32)[:, None]).astype(
        jnp.bfloat16
    )


def pick(selection, values):
    return jnp.dot(selection, values, preferred_element_type=jnp.float32)


def shift_by(values, axis, step):
    size = lax.axis_size(axis)
    return lax.ppermute(values, axis, [(i, (i + step) % size) for i in range(size)])


def sum_direct(part, axis):
    total = part
    for step in range(1, lax.axis_size(axis)):
        total = total + shift_by(part, axis, step)
    return total


def gather_small(part, axis):
    size = lax.axis_size(axis)
    index = lax.axis_index(axis)
    ids = jnp.arange(size, dtype=jnp.int32)[:, None]
    out = jnp.where(ids == index, part[None, :], 0.0)
    for step in range(1, size):
        came = shift_by(part, axis, step)
        out = jnp.where(ids == (index - step) % size, came[None, :], out)
    return out.reshape(-1)


def scatter_direct(partial, axis):
    size = lax.axis_size(axis)
    index = lax.axis_index(axis)
    rows = partial.shape[0] // size

    def piece(owner):
        return lax.dynamic_slice_in_dim(partial, owner * rows, rows)

    total = piece(index).astype(jnp.float32)
    for step in range(1, size):
        came = shift_by(piece((index + step) % size), axis, step)
        total = total + came.astype(jnp.float32)
    return total


def packed_step(cap, sequence_in, operands):
    (
        merger_up,
        merger_up_bias,
        merger_down,
        merger_down_bias,
        norm_gain,
        w_gate,
        w_up,
        hidden_cotangent,
        placement,
        patch_counts,
    ) = operands
    n_row = lax.axis_size("row")
    n_col = lax.axis_size("col")
    col_index = lax.axis_index("col")
    tokens = sequence_in.shape[0]
    held = hidden_cotangent.shape[0]
    packed = cap * n_col
    slot, rank, by_image, extra_slot = pack_plan(
        placement, patch_counts, tokens, n_row, n_col, cap
    )
    arrival = by_image.reshape(n_row, IMG_ROW, n_col, BLK // n_col)
    arrival = jnp.stack(
        [
            lax.dynamic_index_in_dim(arrival, (col_index - step) % n_col, axis=2, keepdims=False)
            for step in range(n_col)
        ],
        axis=1,
    ).reshape(-1)
    sequence = pick(one_hot(arrival, 0, packed), sequence_in).astype(jnp.bfloat16)
    slot_here = lax.dynamic_slice_in_dim(slot, col_index * held, held)
    cotangent = pick(one_hot(slot_here, col_index * cap, cap), hidden_cotangent)
    if cap < held:
        rank_here = lax.dynamic_slice_in_dim(rank, col_index * held, held)
        spilled = pick(one_hot(rank_here, cap, held - cap), hidden_cotangent).astype(jnp.bfloat16)
        spilled_all = lax.all_gather(spilled, "col", axis=0, tiled=True)
        cotangent = cotangent + pick(one_hot(extra_slot, col_index * cap, cap), spilled_all)
    cotangent = cotangent.astype(jnp.bfloat16)

    pre_act = lax.psum_scatter(
        pick(sequence, merger_up).astype(jnp.bfloat16), "col", scatter_dimension=0, tiled=True
    ).astype(jnp.float32) + merger_up_bias.astype(jnp.float32)
    hidden_one = jax.nn.gelu(pre_act, approximate=False).astype(jnp.bfloat16)
    hidden_all = lax.all_gather(hidden_one, "col", axis=0, tiled=True)
    merged_out = lax.optimization_barrier(
        (
            scatter_direct(pick(hidden_all, merger_down).astype(jnp.bfloat16), "row")
            + merger_down_bias.astype(jnp.float32)
        ).astype(jnp.bfloat16)
    )

    def row_sums(part):
        return gather_small(sum_direct(part, "col"), "row")

    merged_f = merged_out.astype(jnp.float32)
    merged_all = lax.all_gather(merged_out, "row", axis=0, tiled=True).astype(jnp.float32)
    square_sums = row_sums(jnp.sum(merged_f * merged_f, axis=1))
    inv_rms = lax.rsqrt(square_sums / D + EPS_NORM)
    gain = norm_gain.astype(jnp.float32)
    normed_all = lax.optimization_barrier(
        (merged_all * inv_rms[:, None] * gain).astype(jnp.bfloat16)
    )

    def block_sums(rows, weight):
        return lax.psum_scatter(
            pick(rows, weight).astype(jnp.bfloat16), "col", scatter_dimension=0, tiled=True
        )

    gate_out = block_sums(normed_all, w_gate)
    up_out = block_sums(normed_all, w_up)
    grad_gate, grad_up = swiglu_grads(gate_out, up_out, cotangent)
    grad_gate_all = lax.all_gather(grad_gate, "col", axis=0, tiled=True)
    grad_up_all = lax.all_gather(grad_up, "col", axis=0, tiled=True)
    from_gate = lax.dot_general(
        grad_gate_all, w_gate, CONTRACT_COLS, preferred_element_type=jnp.float32
    )
    from_up = lax.dot_general(
        grad_up_all, w_up, CONTRACT_COLS, preferred_element_type=jnp.float32
    )
    grad_normed = scatter_direct((from_gate + from_up).astype(jnp.bfloat16), "row").astype(
        jnp.bfloat16
    )
    inner = row_sums(jnp.sum(merged_f * (gain * grad_normed.astype(jnp.float32)), axis=1))
    gained_all = gain * lax.all_gather(grad_normed, "row", axis=0, tiled=True).astype(jnp.float32)
    grad_merged_all = (
        inv_rms[:, None] * gained_all
        - merged_all * (inv_rms * inv_rms * inv_rms / D * inner)[:, None]
    ).astype(jnp.bfloat16)
    grad_hidden = lax.psum_scatter(
        lax.dot_general(
            grad_merged_all, merger_down, CONTRACT_COLS, preferred_element_type=jnp.float32
        ).astype(jnp.bfloat16),
        "col",
        scatter_dimension=0,
        tiled=True,
    ).astype(jnp.float32)
    merger_down_grad = lax.dot_general(
        hidden_all, grad_merged_all, CONTRACT_ROWS, preferred_element_type=jnp.float32
    )
    merger_down_bias_grad = jnp.sum(grad_merged_all, axis=0, dtype=jnp.float32)
    grad_pre = (grad_hidden * gelu_slope(pre_act)).astype(jnp.bfloat16)
    grad_pre_all = lax.all_gather(grad_pre, "col", axis=0, tiled=True)
    merger_up_grad = lax.dot_general(
        sequence, grad_pre_all, CONTRACT_ROWS, preferred_element_type=jnp.float32
    )
    merger_up_bias_grad = jnp.sum(grad_pre_all, axis=0, dtype=jnp.float32)
    return (merger_up_grad, merger_up_bias_grad, merger_down_grad, merger_down_bias_grad)


MESH = pl.DeviceIdType.MESH
F32 = jnp.float32
BF16 = jnp.bfloat16
HALF = 16
SLOTS = 4


def dot_rows(left, right):
    return jnp.dot(left, right, preferred_element_type=F32)


def dot_cols(left, right):
    return lax.dot_general(left, right, CONTRACT_COLS, preferred_element_type=F32)


def tiles_of(width, tile):
    return [(at, min(tile, width - at)) for at in range(0, width, tile)]


def when_in(unit, units, *more):
    ok = (unit >= 0) & (unit < units)
    for cond in more:
        ok = ok & cond
    return pl.when(ok)


class Line:
    def __init__(self, n, units, start, terms, inward, back, sems, credit, finish):
        self.n, self.units, self.start = n, units, start
        self.terms, self.inward, self.back, self.finish = terms, inward, back, finish
        self.sum_send, self.sum_recv, self.back_send, self.back_recv = sems
        self.credit = credit
        self.slots = inward.shape[1]
        self.done = start + 2 * (n - 1)

    def place(self, half):
        me = lax.axis_index("col")
        below, above = jnp.maximum(me - 1, 0), jnp.minimum(me + 1, self.n - 1)
        return (me, above, below) if half == 1 else (self.n - 1 - me, below, above)

    def term(self, half, unit):
        return self.terms.at[lax.rem(unit, self.terms.shape[0]), half]

    def slot(self, half, unit):
        return self.inward.at[half, lax.rem(unit, self.slots)]

    def sum_copy(self, half, unit, first):
        return pltpu.make_async_remote_copy(
            src_ref=self.term(half, unit) if first else self.slot(half, unit),
            dst_ref=self.slot(half, unit),
            send_sem=self.sum_send.at[half, unit],
            recv_sem=self.sum_recv.at[half, unit],
            device_id={"col": self.place(half)[1]},
            device_id_type=MESH,
        )

    def back_copy(self, half, unit):
        return pltpu.make_async_remote_copy(
            src_ref=self.back.at[unit, half],
            dst_ref=self.back.at[unit, half],
            send_sem=self.back_send.at[half, unit],
            recv_sem=self.back_recv.at[half, unit],
            device_id={"col": self.place(half)[2]},
            device_id_type=MESH,
        )

    def free(self, half, unit):
        @pl.when(unit + self.slots < self.units)
        def _():
            pl.semaphore_signal(
                self.credit.at[half],
                inc=1,
                device_id={"col": self.place(half)[2]},
                device_id_type=MESH,
            )

    def sums(self, tick):
        n = self.n
        for half in (0, 1):
            hops = self.place(half)[0]
            unit = tick - self.start - hops
            sent = unit - 2

            @when_in(sent, self.units, hops < n - 1)
            def _():
                self.sum_copy(half, sent, False).wait_send()

                @pl.when(hops > 0)
                def _():
                    self.free(half, sent)

            @when_in(unit, self.units, hops > 0)
            def _():
                self.sum_copy(half, unit, False).wait_recv()

            @when_in(unit, self.units, hops > 0, hops < n - 1)
            def _():
                slot = self.slot(half, unit)
                slot[...] = (
                    slot[...].astype(F32) + self.term(half, unit)[...].astype(F32)
                ).astype(BF16)

            @when_in(unit, self.units, hops < n - 1, unit >= self.slots)
            def _():
                pl.semaphore_wait(self.credit.at[half], 1)

            @when_in(unit, self.units, hops == 0)
            def _():
                self.sum_copy(half, unit, True).start()

            @when_in(unit, self.units, hops > 0, hops < n - 1)
            def _():
                self.sum_copy(half, unit, False).start()

            @when_in(unit, self.units, hops == n - 1)
            def _():
                self.finish(
                    half,
                    unit,
                    self.slot(half, unit),
                    self.term(half, unit),
                    self.back.at[unit, half],
                )
                self.back_copy(half, unit).start()
                self.free(half, unit)

    def backs(self, tick):
        for half in (0, 1):
            hops = self.place(half)[0]
            unit = tick - self.done + hops

            @when_in(unit, self.units, hops < self.n - 1)
            def _():
                self.back_copy(half, unit).wait_recv()

            @when_in(unit, self.units, hops < self.n - 1, hops > 0)
            def _():
                self.back_copy(half, unit).start()

    def drain(self):
        @pl.loop(0, self.units)
        def _(unit):
            for half in (0, 1):

                @pl.when(self.place(half)[0] > 0)
                def _():
                    self.back_copy(half, unit).wait_send()


class RowSum:
    def __init__(self, chips, units, start, buf, stage, core_in, chip_in, sems, finish):
        self.chips, self.units, self.start = chips, units, start
        self.buf, self.stage, self.core_in, self.chip_in = buf, stage, core_in, chip_in
        self.finish = finish
        self.s1, self.r1, self.s2, self.r2, self.s3, self.r3 = sems
        self.done = start + 3
        row = lax.axis_index("row")
        self.core = lax.rem(row, 2)
        self.other = 1 - self.core
        self.chip = lax.div(row, 2)
        self.partner = self.chip * 2 + self.other

    def first(self, unit):
        return pltpu.make_async_remote_copy(
            src_ref=self.stage.at[lax.rem(unit, 2)],
            dst_ref=self.core_in.at[unit],
            send_sem=self.s1.at[unit],
            recv_sem=self.r1.at[unit],
            device_id={"row": self.partner},
            device_id_type=MESH,
        )

    def second(self, unit, step):
        return pltpu.make_async_remote_copy(
            src_ref=self.buf.at[unit, self.core],
            dst_ref=self.chip_in.at[unit, step - 1],
            send_sem=self.s2.at[unit, step - 1],
            recv_sem=self.r2.at[unit, step - 1],
            device_id={"row": lax.rem(self.chip + step, self.chips) * 2 + self.core},
            device_id_type=MESH,
        )

    def third(self, unit, half):
        return pltpu.make_async_remote_copy(
            src_ref=self.buf.at[unit, half],
            dst_ref=self.buf.at[unit, half],
            send_sem=self.s3.at[unit],
            recv_sem=self.r3.at[unit],
            device_id={"row": self.partner},
            device_id_type=MESH,
        )

    def begin(self, tick):
        unit = tick - self.start

        @when_in(unit, self.units)
        def _():
            self.stage[lax.rem(unit, 2)] = self.buf[unit, self.other]
            self.first(unit).start()

    def steps(self, tick):
        core, chips = self.core, self.chips
        unit1 = tick - self.start - 1

        @when_in(unit1, self.units)
        def _():
            self.first(unit1).wait_recv()
            self.buf[unit1, core] = (
                self.buf[unit1, core].astype(F32) + self.core_in[unit1].astype(F32)
            ).astype(BF16)
            for step in range(1, chips):
                self.second(unit1, step).start()

        unit2 = tick - self.start - 2

        @when_in(unit2, self.units)
        def _():
            total = self.buf[unit2, core].astype(F32)
            for step in range(1, chips):
                self.second(unit2, step).wait_recv()
                total = total + self.chip_in[unit2, step - 1].astype(F32)
            for step in range(1, chips):
                self.second(unit2, step).wait_send()
            self.buf[unit2, core] = self.finish(total)
            self.first(unit2).wait_send()
            self.third(unit2, core).start()

        unit3 = tick - self.start - 3

        @when_in(unit3, self.units)
        def _():
            self.third(unit3, self.other).wait_recv()
            self.third(unit3, core).wait_send()


class Shares:
    def __init__(self, n, buf, sems):
        self.n, self.buf = n, buf
        self.send, self.recv = sems

    def copy(self, unit, step, arriving=False):
        me = lax.axis_index("col")
        slot = lax.rem(me + self.n - step, self.n) if arriving else me
        return pltpu.make_async_remote_copy(
            src_ref=self.buf.at[unit, slot],
            dst_ref=self.buf.at[unit, slot],
            send_sem=self.send.at[unit, step - 1],
            recv_sem=self.recv.at[unit, step - 1],
            device_id={"col": lax.rem(me + step, self.n)},
            device_id_type=MESH,
        )

    def put(self, unit, column):
        me = lax.axis_index("col")
        self.buf[unit, me] = jnp.broadcast_to(column, self.buf.shape[2:])
        for step in range(1, self.n):
            self.copy(unit, step).start()

    def wait(self, unit):
        for step in range(1, self.n):
            self.copy(unit, step, True).wait_recv()
            self.copy(unit, step).wait_send()

    def total(self, unit, rows=slice(None)):
        total = self.buf[unit, 0, rows]
        for index in range(1, self.n):
            total = total + self.buf[unit, index, rows]
        return total[:, :1]


def chain_kernel(
    n,
    chips,
    units,
    seq_ref,
    up_bias_ref,
    down_bias_ref,
    gain_ref,
    cot_ref,
    up_hbm,
    down_hbm,
    wg_hbm,
    wu_hbm,
    hidden_hbm,
    grad_merged_hbm,
    grad_pre_hbm,
    w_up_v,
    w_down_v,
    wg_v,
    wu_v,
    b_terms,
    b_in,
    b_back,
    pre_act,
    c_buf,
    c_stage,
    core_in,
    c_chip,
    squares,
    d_terms,
    d_in,
    d_back,
    e_buf,
    e_stage,
    e_chip,
    inners,
    f_terms,
    f_in,
    f_back,
    w_sems,
    b_sems,
    d_sems,
    f_sems,
    credits,
    c_sem1,
    c_sem2,
    c_sem3,
    e_sem1,
    e_sem2,
    e_sem3,
    sq_sems,
    in_sems,
    out_sems,
):
    me = lax.axis_index("col")
    row = lax.axis_index("row")
    core = lax.rem(row, 2)
    chip = lax.div(row, 2)
    m = HALF
    rows = 2 * m

    loads = [
        pltpu.make_async_copy(src, dst, w_sems.at[k])
        for k, (src, dst) in enumerate(
            [(up_hbm, w_up_v), (down_hbm, w_down_v), (wg_hbm, wg_v), (wu_hbm, wu_v)]
        )
    ]
    for load in loads:
        load.start()

    barrier = pltpu.get_barrier_semaphore()
    for step in range(1, n):
        pl.semaphore_signal(
            barrier, inc=1, device_id={"col": lax.rem(me + step, n)}, device_id_type=MESH
        )
    pl.semaphore_signal(
        barrier, inc=1, device_id={"row": chip * 2 + 1 - core}, device_id_type=MESH
    )
    for step in range(1, chips):
        pl.semaphore_signal(
            barrier,
            inc=1,
            device_id={"row": lax.rem(chip + step, chips) * 2 + core},
            device_id_type=MESH,
        )
    pl.semaphore_wait(barrier, n - 1 + chips)

    def gelu_finish(half, unit, came, term, out):
        value = came[0].astype(F32) + term[0].astype(F32) + up_bias_ref[...]
        pre_act[unit] = value
        out[0] = (0.5 * value * (1.0 + lax.erf(value / math.sqrt(2.0)))).astype(BF16)

    def swiglu_finish(half, unit, came, term, out):
        inv = lax.rsqrt(squares_io.total(unit, slice(half * m, (half + 1) * m)) / D + EPS_NORM)
        gate = ((came[0].astype(F32) + term[0].astype(F32)) * inv).astype(BF16).astype(F32)
        up = ((came[1].astype(F32) + term[1].astype(F32)) * inv).astype(BF16).astype(F32)
        masked = cot_ref[unit].astype(F32)
        logistic = 1.0 / (1.0 + jnp.exp(-gate))
        through = masked * logistic
        out[0] = (through * up * (1.0 + gate * (1.0 - logistic))).astype(BF16)
        out[1] = (through * gate).astype(BF16)

    def slope_finish(half, unit, came, term, out):
        value = came[0].astype(F32) + term[0].astype(F32)
        out[0] = (value * gelu_slope(pre_act[unit])).astype(BF16)

    def parts(sems, count):
        return [sems.at[k] for k in range(count)]

    squares_io = Shares(n, squares, parts(sq_sems, 2))
    inners_io = Shares(n, inners, parts(in_sems, 2))
    line_b = Line(
        n, units, 0, b_terms, b_in, b_back, parts(b_sems, 4), credits.at[0], gelu_finish
    )
    sum_c = RowSum(
        chips,
        units,
        line_b.done,
        c_buf,
        c_stage,
        core_in,
        c_chip,
        parts(c_sem1, 2) + parts(c_sem2, 2) + parts(c_sem3, 2),
        lambda total: (total + down_bias_ref[...]).astype(BF16),
    )
    line_d = Line(
        n,
        units,
        sum_c.done + 2,
        d_terms,
        d_in,
        d_back,
        parts(d_sems, 4),
        credits.at[1],
        swiglu_finish,
    )
    sum_e = RowSum(
        chips,
        units,
        line_d.done + 2,
        e_buf,
        e_stage,
        core_in,
        e_chip,
        parts(e_sem1, 2) + parts(e_sem2, 2) + parts(e_sem3, 2),
        lambda total: total.astype(BF16),
    )
    line_f = Line(
        n,
        units,
        sum_e.done + 1,
        f_terms,
        f_in,
        f_back,
        parts(f_sems, 4),
        credits.at[2],
        slope_finish,
    )
    ticks = units + line_f.done + 1

    def out_copies(unit):
        return [
            pltpu.make_async_copy(src.at[unit], dst.at[unit], out_sems.at[k, unit])
            for k, (src, dst) in enumerate(
                [(b_back, hidden_hbm), (e_buf, grad_merged_hbm), (f_back, grad_pre_hbm)]
            )
        ]

    def tick_body(tick, carry):
        unit_q = tick - (sum_c.done + 1)

        @when_in(unit_q, units)
        def _():
            squares_io.wait(unit_q)

        line_d.sums(tick)
        line_d.backs(tick)

        unit_f = tick - line_f.start

        @when_in(unit_f, units)
        def _():
            inners_io.wait(unit_f)
            inv = lax.rsqrt(squares_io.total(unit_f) / D + EPS_NORM)
            factor = inv * inv * inv / D * inners_io.total(unit_f)
            merged = c_buf[unit_f].reshape(rows, -1).astype(F32)
            gained = e_buf[unit_f].reshape(rows, -1).astype(F32) * gain_ref[...]
            grad = (inv * gained - merged * factor).astype(BF16)
            e_buf[unit_f] = grad.reshape(2, m, -1)
            out_copies(unit_f)[1].start()
            slot = lax.rem(unit_f, n)
            for at, size in tiles_of(w_down_v.shape[0], 640):
                part = dot_cols(grad, w_down_v[pl.ds(at, size), :]).astype(BF16)
                f_terms[slot, :, 0, :, pl.ds(at, size)] = part.reshape(2, m, size)

        line_f.sums(tick)
        line_f.backs(tick)

        unit_z = tick - line_f.done

        @when_in(unit_z, units)
        def _():
            out_copies(unit_z)[2].start()

        sum_e.steps(tick)
        unit_i = tick - sum_e.done

        @when_in(unit_i, units)
        def _():
            merged = c_buf[unit_i].reshape(rows, -1).astype(F32)
            gained = e_buf[unit_i].reshape(rows, -1).astype(F32) * gain_ref[...]
            inners_io.put(unit_i, jnp.sum(merged * gained, axis=1, keepdims=True))

        sum_c.steps(tick)

        unit_s = tick - sum_c.done

        @when_in(unit_s, units)
        def _():
            merged = c_buf[unit_s].reshape(rows, -1).astype(F32)
            squares_io.put(unit_s, jnp.sum(merged * merged, axis=1, keepdims=True))

        @pl.when(tick == 0)
        def _():
            loads[0].wait()

        unit_b = tick

        @when_in(unit_b, units)
        def _():
            slot = lax.rem(unit_b, n)
            seq = seq_ref[unit_b].reshape(rows, -1)
            for at, size in tiles_of(w_up_v.shape[1], 640):
                part = dot_rows(seq, w_up_v[:, pl.ds(at, size)]).astype(BF16)
                b_terms[slot, :, 0, :, pl.ds(at, size)] = part.reshape(2, m, size)

        line_b.sums(tick)
        line_b.backs(tick)

        @pl.when(tick == sum_c.start)
        def _():
            loads[1].wait()

        unit_c = tick - sum_c.start

        @when_in(unit_c, units)
        def _():
            out_copies(unit_c)[0].start()
            hidden = b_back[unit_c, :, 0].reshape(rows, -1)
            for at, size in tiles_of(w_down_v.shape[1], 512):
                part = dot_rows(hidden, w_down_v[:, pl.ds(at, size)]).astype(BF16)
                c_buf[unit_c, :, :, pl.ds(at, size)] = part.reshape(2, m, size)

        sum_c.begin(tick)

        unit_e = tick - line_d.done - 2

        @when_in(unit_e, units, lax.rem(unit_e, 2) == 0)
        def _():
            pair = pl.ds(unit_e, 2)
            grad_gate = d_back[pair, :, 0].reshape(2 * rows, -1)
            grad_up = d_back[pair, :, 1].reshape(2 * rows, -1)
            for at, size in tiles_of(wg_v.shape[1], 512):
                part = (
                    dot_rows(grad_gate, wg_v[:, pl.ds(at, size)])
                    + dot_rows(grad_up, wu_v[:, pl.ds(at, size)])
                ).astype(BF16)
                e_buf[pair, :, :, pl.ds(at, size)] = part.reshape(2, 2, m, size)

        sum_e.begin(tick)

        @pl.when(tick == sum_c.done + 1)
        def _():
            loads[2].wait()
            loads[3].wait()

        unit_d = tick - sum_c.done - 1

        @when_in(unit_d, units, lax.rem(unit_d, 2) == 0)
        def _():
            merged = c_buf[pl.ds(unit_d, 2)].reshape(2 * rows, -1).astype(F32)
            lifted = (merged * gain_ref[...]).astype(BF16)
            slots = [lax.rem(unit_d + k, d_terms.shape[0]) for k in range(2)]
            for plane, weight in enumerate((wg_v, wu_v)):
                for at, size in tiles_of(weight.shape[0], 1024):
                    part = dot_cols(lifted, weight[pl.ds(at, size), :]).astype(BF16)
                    part = part.reshape(2, 2, m, size)
                    for k in range(2):
                        d_terms[slots[k], :, plane, :, pl.ds(at, size)] = part[k]

        return carry

    lax.fori_loop(0, ticks, tick_body, 0)
    line_b.drain()
    line_d.drain()
    line_f.drain()

    @pl.loop(0, units)
    def _(unit):
        for copy in out_copies(unit):
            copy.wait()


def chain(units, branch_id, seq, cot, operands):
    (
        merger_up,
        merger_up_bias,
        merger_down,
        merger_down_bias,
        norm_gain,
        w_gate,
        w_up,
    ) = operands
    n = lax.axis_size("col")
    chips = lax.axis_size("row") // 2
    m = HALF
    mdim, hid = merger_up.shape
    width = merger_down.shape[1]
    ffw = w_gate.shape[1]
    vmem = pl.BlockSpec(memory_space=pltpu.VMEM)
    hbm = pl.BlockSpec(memory_space=pltpu.HBM)
    dma = pltpu.SemaphoreType.DMA
    flops = 2 * units * 2 * m * (mdim * hid + 2 * hid * width + 4 * width * ffw)
    return pl.pallas_call(
        functools.partial(chain_kernel, n, chips, units),
        out_shape=[
            jax.ShapeDtypeStruct((units, 2, 1, m, hid), BF16),
            jax.ShapeDtypeStruct((units, 2, m, width), BF16),
            jax.ShapeDtypeStruct((units, 2, 1, m, hid), BF16),
        ],
        in_specs=[vmem] * 5 + [hbm] * 4,
        out_specs=[hbm] * 3,
        scratch_shapes=[
            pltpu.VMEM(merger_up.shape, BF16),
            pltpu.VMEM(merger_down.shape, BF16),
            pltpu.VMEM((ffw, width), BF16),
            pltpu.VMEM((ffw, width), BF16),
            pltpu.VMEM((n, 2, 1, m, hid), BF16),
            pltpu.VMEM((2, SLOTS, 1, m, hid), BF16),
            pltpu.VMEM((units, 2, 1, m, hid), BF16),
            pltpu.VMEM((units, m, hid), F32),
            pltpu.VMEM((units, 2, m, width), BF16),
            pltpu.VMEM((2, m, width), BF16),
            pltpu.VMEM((units, m, width), BF16),
            pltpu.VMEM((units, chips - 1, m, width), BF16),
            pltpu.VMEM((units, n, 2 * m, 128), F32),
            pltpu.VMEM((n + 1, 2, 2, m, ffw), BF16),
            pltpu.VMEM((2, SLOTS, 2, m, ffw), BF16),
            pltpu.VMEM((units, 2, 2, m, ffw), BF16),
            pltpu.VMEM((units, 2, m, width), BF16),
            pltpu.VMEM((2, m, width), BF16),
            pltpu.VMEM((units, chips - 1, m, width), BF16),
            pltpu.VMEM((units, n, 2 * m, 128), F32),
            pltpu.VMEM((n, 2, 1, m, hid), BF16),
            pltpu.VMEM((2, SLOTS, 1, m, hid), BF16),
            pltpu.VMEM((units, 2, 1, m, hid), BF16),
            dma((4,)),
            dma((4, 2, units)),
            dma((4, 2, units)),
            dma((4, 2, units)),
            pltpu.SemaphoreType.REGULAR((3, 2)),
            dma((2, units)),
            dma((2, units, chips - 1)),
            dma((2, units)),
            dma((2, units)),
            dma((2, units, chips - 1)),
            dma((2, units)),
            dma((2, units, n - 1)),
            dma((2, units, n - 1)),
            dma((3, units)),
        ],
        cost_estimate=pl.CostEstimate(
            flops=flops, bytes_accessed=2 * (mdim * hid + hid * width + 2 * width * ffw),
            transcendentals=units * m * ffw,
        ),
        compiler_params=pltpu.CompilerParams(
            collective_id=branch_id, has_side_effects=True, vmem_limit_bytes=63 * 1024 * 1024
        ),
    )(
        seq,
        merger_up_bias.astype(F32)[None],
        merger_down_bias.astype(F32)[None],
        norm_gain.astype(F32)[None],
        cot,
        merger_up,
        merger_down,
        w_gate.T,
        w_up.T,
    )


def half_plan(placement, patch_counts, tokens, n_col):
    images = placement.shape[0]
    ids = jnp.arange(images, dtype=jnp.int32)
    hit = placement[:, None] == ids[None, :]
    fill = jnp.sum(jnp.where(hit, (patch_counts // 4)[:, None], 0), axis=0)
    half = ids // (images // 2)
    before = (half[:, None] == half[None, :]) & (ids[None, :] < ids[:, None])
    start = jnp.sum(jnp.where(before, fill[None, :], 0), axis=1)
    place = jnp.arange(BLK, dtype=jnp.int32)
    rank = start[:, None] + place[None, :]
    real = place[None, :] < fill[:, None]
    slot = (rank // HALF) * (2 * HALF) + half[:, None] * HALF + rank % HALF
    slot = jnp.where(real, slot, -1)
    rank = jnp.where(real, rank, -1)
    by_image = jnp.sum(jnp.where(hit[:, :, None], slot[None, :, :], 0), axis=1)
    return rank.reshape(n_col, -1), by_image


def half_step(units, branch_id, sequence_in, cot_near, operands):
    (
        merger_up,
        merger_up_bias,
        merger_down,
        merger_down_bias,
        norm_gain,
        w_gate,
        w_up,
        hidden_cotangent,
        placement,
        patch_counts,
    ) = operands
    n_row = lax.axis_size("row")
    n_col = lax.axis_size("col")
    col_index = lax.axis_index("col")
    tokens = sequence_in.shape[0]
    rank, by_image = half_plan(placement, patch_counts, tokens, n_col)
    arrival = by_image.reshape(n_row, IMG_ROW, n_col, BLK // n_col)
    arrival = jnp.stack(
        [
            lax.dynamic_index_in_dim(arrival, (col_index - step) % n_col, axis=2, keepdims=False)
            for step in range(n_col)
        ],
        axis=1,
    ).reshape(-1)
    packed = units * 2 * HALF
    sequence = pick(one_hot(arrival, 0, packed), sequence_in).astype(BF16)
    near = n_col // 2
    rank_here = jnp.where(col_index >= near, rank[::-1][:near], rank[:near]).reshape(-1)
    cot = pick(one_hot(rank_here, 0, units * HALF), cot_near).astype(BF16)
    hidden_all, grad_merged_all, grad_pre_all = chain(
        units,
        branch_id,
        sequence.reshape(units, 2, HALF, -1),
        cot.reshape(units, HALF, -1),
        operands[:7],
    )
    hidden_all = hidden_all.reshape(packed, -1)
    grad_merged_all = grad_merged_all.reshape(packed, -1)
    grad_pre_all = grad_pre_all.reshape(packed, -1)
    merger_down_grad = lax.dot_general(
        hidden_all, grad_merged_all, CONTRACT_ROWS, preferred_element_type=F32
    )
    merger_down_bias_grad = jnp.sum(grad_merged_all, axis=0, dtype=F32)
    merger_up_grad = lax.dot_general(
        sequence, grad_pre_all, CONTRACT_ROWS, preferred_element_type=F32
    )
    merger_up_bias_grad = jnp.sum(grad_pre_all, axis=0, dtype=F32)
    return (merger_up_grad, merger_up_bias_grad, merger_down_grad, merger_down_bias_grad)


def shards(
    patches,
    patch_gain,
    patch_bias,
    merger_up,
    merger_up_bias,
    merger_down,
    merger_down_bias,
    norm_gain,
    w_gate,
    w_up,
    hidden_cotangent,
    placement,
    patch_counts,
):
    n_col = lax.axis_size("col")
    held = hidden_cotangent.shape[0]
    images = placement.shape[0]
    half_of = placement // (images // 2)
    in_half = jnp.where(
        half_of[:, None] == jnp.arange(2)[None, :], (patch_counts // 4)[:, None], 0
    )
    own_rows = jnp.max(jnp.sum(in_half, axis=0))
    real_rows = own_rows
    for step in range(1, lax.axis_size("group")):
        real_rows = jnp.maximum(real_rows, shift_by(own_rows, "group", step))
    most = held * n_col // 2 // HALF
    counts = [most * 5 // 8, most * 3 // 4]
    branch = sum((real_rows > units * HALF).astype(jnp.int32) for units in counts)
    near = [hidden_cotangent]
    for step in range(1, n_col // 2):
        near.append(
            lax.ppermute(hidden_cotangent, "col", [(step, 0), (n_col - 1 - step, n_col - 1)])
        )
    cot_near = jnp.concatenate(near, axis=0)
    image_tokens = patch_tokens(patches, patch_gain, patch_bias)
    slot_count = image_tokens.shape[1]
    feat_width = image_tokens.shape[2] // n_col
    sending = image_tokens.reshape(IMG_ROW * slot_count, n_col, feat_width)
    sending = jnp.transpose(sending, (1, 0, 2))
    col_index = lax.axis_index("col")
    pieces = [lax.dynamic_index_in_dim(sending, col_index, keepdims=False)]
    for step in range(1, n_col):
        outgoing = lax.dynamic_index_in_dim(
            sending, (col_index + step) % n_col, keepdims=False
        )
        pieces.append(shift_by(outgoing, "col", step))
    merged = jnp.concatenate(pieces, axis=0)
    gathered_in = lax.all_gather(merged, "row", axis=0, tiled=True)
    operands = (
        merger_up,
        merger_up_bias,
        merger_down,
        merger_down_bias,
        norm_gain,
        w_gate,
        w_up,
        hidden_cotangent,
        placement,
        patch_counts,
    )
    steps = [
        functools.partial(half_step, units, number) for number, units in enumerate(counts)
    ]

    def whole_step(sequence_in, cot_near, operands):
        return packed_step(held, sequence_in, operands)

    return lax.switch(branch, steps + [whole_step], gathered_in, cot_near, operands)


def solution(mesh):
    in_specs = (
        P(("group", "row"), "col", None),
        P(),
        P(),
        P("col", "row"),
        P("row"),
        P("row", "col"),
        P("col"),
        P("col"),
        P("col", "row"),
        P("col", "row"),
        P(("group", "col"), "row"),
        P("group"),
        P("group"),
    )
    out_specs = (
        P(("group", "col"), "row"),
        P(("group", "row")),
        P(("group", "row"), "col"),
        P(("group", "col")),
    )
    return jax.shard_map(shards, mesh=mesh, in_specs=in_specs, out_specs=out_specs, check_vma=False)
```

```python
import functools
import math

import jax
import jax.numpy as jnp
from jax import lax
from jax.experimental import pallas as pl
from jax.experimental.pallas import tpu as pltpu
from jax.sharding import PartitionSpec as P

D = 8192
BLK = 16
IMG_ROW = 8


EPS_PATCH = 1e-06
EPS_NORM = 1e-06
CONTRACT_ROWS = (((0,), (0,)), ((), ()))
CONTRACT_COLS = (((1,), (1,)), ((), ()))


def gelu_slope(inputs):
    cumulative = 0.5 * (1.0 + jax.scipy.special.erf(inputs / math.sqrt(2.0)))
    return cumulative + inputs * jnp.exp(-0.5 * inputs * inputs) / math.sqrt(2.0 * math.pi)


def patch_tokens(patches, patch_gain, patch_bias):
    values = patches.astype(jnp.float32)
    center = values - jnp.mean(values, axis=-1, keepdims=True)
    spread = jnp.mean(center * center, axis=-1, keepdims=True)
    normed = center * lax.rsqrt(spread + EPS_PATCH) * patch_gain.astype(
        jnp.float32
    ) + patch_bias.astype(jnp.float32)
    image_count, patch_slots, patch_width = patches.shape
    return normed.astype(jnp.bfloat16).reshape(image_count, patch_slots // 4, 4 * patch_width)


def swiglu_grads(gate_out, up_out, cotangent):
    gate_f = gate_out.astype(jnp.float32)
    up_f = up_out.astype(jnp.float32)
    masked = cotangent.astype(jnp.float32)
    logistic = jax.nn.sigmoid(gate_f)
    grad_gate = (masked * up_f * logistic * (1.0 + gate_f * (1.0 - logistic))).astype(jnp.bfloat16)
    grad_up = (masked * gate_f * logistic).astype(jnp.bfloat16)
    return (grad_gate, grad_up)


def pack_plan(placement, patch_counts, tokens, n_row, n_col, cap):
    images = placement.shape[0]
    rows = tokens // n_col
    blocks = rows // BLK
    ids = jnp.arange(images, dtype=jnp.int32)
    cols = jnp.arange(n_col, dtype=jnp.int32)
    hit = placement[:, None] == ids[None, :]
    fill = jnp.sum(jnp.where(hit, (patch_counts // 4)[:, None], 0), axis=0)
    owner = ids // blocks
    before = (owner[:, None] == owner[None, :]) & (ids[None, :] < ids[:, None])
    start = jnp.sum(jnp.where(before, fill[None, :], 0), axis=1)
    count = jnp.sum(jnp.where(owner[None, :] == cols[:, None], fill[None, :], 0), axis=1)
    over = jnp.maximum(count - cap, 0)
    free = jnp.maximum(cap - count, 0)
    lower = cols[None, :] < cols[:, None]
    over_start = jnp.sum(jnp.where(lower, over[None, :], 0), axis=1)
    free_start = jnp.sum(jnp.where(lower, free[None, :], 0), axis=1)

    def spill_slot(number):
        inside = (number[..., None] >= free_start) & (number[..., None] < free_start + free)
        return jnp.sum(
            jnp.where(inside, cols * cap + count + number[..., None] - free_start, 0), axis=-1
        )

    place = jnp.arange(BLK, dtype=jnp.int32)
    rank = start[:, None] + place[None, :]
    real = place[None, :] < fill[:, None]
    owner_over = jnp.sum(jnp.where(owner[:, None] == cols[None, :], over_start[None, :], 0), axis=1)
    slot = jnp.where(
        rank < cap,
        owner[:, None] * cap + rank,
        spill_slot(owner_over[:, None] + rank - cap),
    )
    slot = jnp.where(real, slot, -1)
    rank = jnp.where(real, rank, -1)
    by_image = jnp.sum(jnp.where(hit[:, :, None], slot[None, :, :], 0), axis=1)
    extra = jnp.arange(rows - cap, dtype=jnp.int32)
    extra_slot = jnp.where(
        extra[None, :] < over[:, None], spill_slot(over_start[:, None] + extra[None, :]), -1
    )
    return slot.reshape(-1), rank.reshape(-1), by_image, extra_slot.reshape(-1)


def one_hot(slots, first, size):
    return (slots[None, :] - first == jnp.arange(size, dtype=jnp.int32)[:, None]).astype(
        jnp.bfloat16
    )


def pick(selection, values):
    return jnp.dot(selection, values, preferred_element_type=jnp.float32)


def shift_by(values, axis, step):
    size = lax.axis_size(axis)
    return lax.ppermute(values, axis, [(i, (i + step) % size) for i in range(size)])


def sum_direct(part, axis):
    total = part
    for step in range(1, lax.axis_size(axis)):
        total = total + shift_by(part, axis, step)
    return total


def gather_small(part, axis):
    size = lax.axis_size(axis)
    index = lax.axis_index(axis)
    ids = jnp.arange(size, dtype=jnp.int32)[:, None]
    out = jnp.where(ids == index, part[None, :], 0.0)
    for step in range(1, size):
        came = shift_by(part, axis, step)
        out = jnp.where(ids == (index - step) % size, came[None, :], out)
    return out.reshape(-1)


def scatter_direct(partial, axis):
    size = lax.axis_size(axis)
    index = lax.axis_index(axis)
    rows = partial.shape[0] // size

    def piece(owner):
        return lax.dynamic_slice_in_dim(partial, owner * rows, rows)

    total = piece(index).astype(jnp.float32)
    for step in range(1, size):
        came = shift_by(piece((index + step) % size), axis, step)
        total = total + came.astype(jnp.float32)
    return total


def packed_step(cap, sequence_in, operands):
    (
        merger_up,
        merger_up_bias,
        merger_down,
        merger_down_bias,
        norm_gain,
        w_gate,
        w_up,
        hidden_cotangent,
        placement,
        patch_counts,
    ) = operands
    n_row = lax.axis_size("row")
    n_col = lax.axis_size("col")
    col_index = lax.axis_index("col")
    tokens = sequence_in.shape[0]
    held = hidden_cotangent.shape[0]
    packed = cap * n_col
    slot, rank, by_image, extra_slot = pack_plan(
        placement, patch_counts, tokens, n_row, n_col, cap
    )
    arrival = by_image.reshape(n_row, IMG_ROW, n_col, BLK // n_col)
    arrival = jnp.stack(
        [
            lax.dynamic_index_in_dim(arrival, (col_index - step) % n_col, axis=2, keepdims=False)
            for step in range(n_col)
        ],
        axis=1,
    ).reshape(-1)
    sequence = pick(one_hot(arrival, 0, packed), sequence_in).astype(jnp.bfloat16)
    slot_here = lax.dynamic_slice_in_dim(slot, col_index * held, held)
    cotangent = pick(one_hot(slot_here, col_index * cap, cap), hidden_cotangent)
    if cap < held:
        rank_here = lax.dynamic_slice_in_dim(rank, col_index * held, held)
        spilled = pick(one_hot(rank_here, cap, held - cap), hidden_cotangent).astype(jnp.bfloat16)
        spilled_all = lax.all_gather(spilled, "col", axis=0, tiled=True)
        cotangent = cotangent + pick(one_hot(extra_slot, col_index * cap, cap), spilled_all)
    cotangent = cotangent.astype(jnp.bfloat16)

    pre_act = lax.psum_scatter(
        pick(sequence, merger_up).astype(jnp.bfloat16), "col", scatter_dimension=0, tiled=True
    ).astype(jnp.float32) + merger_up_bias.astype(jnp.float32)
    hidden_one = jax.nn.gelu(pre_act, approximate=False).astype(jnp.bfloat16)
    hidden_all = lax.all_gather(hidden_one, "col", axis=0, tiled=True)
    merged_out = lax.optimization_barrier(
        (
            scatter_direct(pick(hidden_all, merger_down).astype(jnp.bfloat16), "row")
            + merger_down_bias.astype(jnp.float32)
        ).astype(jnp.bfloat16)
    )

    def row_sums(part):
        return gather_small(sum_direct(part, "col"), "row")

    merged_f = merged_out.astype(jnp.float32)
    merged_all = lax.all_gather(merged_out, "row", axis=0, tiled=True).astype(jnp.float32)
    square_sums = row_sums(jnp.sum(merged_f * merged_f, axis=1))
    inv_rms = lax.rsqrt(square_sums / D + EPS_NORM)
    gain = norm_gain.astype(jnp.float32)
    normed_all = lax.optimization_barrier(
        (merged_all * inv_rms[:, None] * gain).astype(jnp.bfloat16)
    )

    def block_sums(rows, weight):
        return lax.psum_scatter(
            pick(rows, weight).astype(jnp.bfloat16), "col", scatter_dimension=0, tiled=True
        )

    gate_out = block_sums(normed_all, w_gate)
    up_out = block_sums(normed_all, w_up)
    grad_gate, grad_up = swiglu_grads(gate_out, up_out, cotangent)
    grad_gate_all = lax.all_gather(grad_gate, "col", axis=0, tiled=True)
    grad_up_all = lax.all_gather(grad_up, "col", axis=0, tiled=True)
    from_gate = lax.dot_general(
        grad_gate_all, w_gate, CONTRACT_COLS, preferred_element_type=jnp.float32
    )
    from_up = lax.dot_general(
        grad_up_all, w_up, CONTRACT_COLS, preferred_element_type=jnp.float32
    )
    grad_normed = scatter_direct((from_gate + from_up).astype(jnp.bfloat16), "row").astype(
        jnp.bfloat16
    )
    inner = row_sums(jnp.sum(merged_f * (gain * grad_normed.astype(jnp.float32)), axis=1))
    gained_all = gain * lax.all_gather(grad_normed, "row", axis=0, tiled=True).astype(jnp.float32)
    grad_merged_all = (
        inv_rms[:, None] * gained_all
        - merged_all * (inv_rms * inv_rms * inv_rms / D * inner)[:, None]
    ).astype(jnp.bfloat16)
    grad_hidden = lax.psum_scatter(
        lax.dot_general(
            grad_merged_all, merger_down, CONTRACT_COLS, preferred_element_type=jnp.float32
        ).astype(jnp.bfloat16),
        "col",
        scatter_dimension=0,
        tiled=True,
    ).astype(jnp.float32)
    merger_down_grad = lax.dot_general(
        hidden_all, grad_merged_all, CONTRACT_ROWS, preferred_element_type=jnp.float32
    )
    merger_down_bias_grad = jnp.sum(grad_merged_all, axis=0, dtype=jnp.float32)
    grad_pre = (grad_hidden * gelu_slope(pre_act)).astype(jnp.bfloat16)
    grad_pre_all = lax.all_gather(grad_pre, "col", axis=0, tiled=True)
    merger_up_grad = lax.dot_general(
        sequence, grad_pre_all, CONTRACT_ROWS, preferred_element_type=jnp.float32
    )
    merger_up_bias_grad = jnp.sum(grad_pre_all, axis=0, dtype=jnp.float32)
    return (merger_up_grad, merger_up_bias_grad, merger_down_grad, merger_down_bias_grad)


MESH = pl.DeviceIdType.MESH
F32 = jnp.float32
BF16 = jnp.bfloat16
HALF = 16
SLOTS = 4
ROW_SLOTS = 3
SPILL = 32
SIXTEENTHS = (9, 10, 11)


def dot_rows(left, right):
    return jnp.dot(left, right, preferred_element_type=F32)


def dot_cols(left, right):
    return lax.dot_general(left, right, CONTRACT_COLS, preferred_element_type=F32)


def tiles_of(width, tile):
    return [(at, min(tile, width - at)) for at in range(0, width, tile)]


def when_in(unit, units, *more):
    ok = (unit >= 0) & (unit < units)
    for cond in more:
        ok = ok & cond
    return pl.when(ok)


class Line:
    def __init__(self, n, units, start, split, bufs, sems, credit, finish):
        self.n, self.units, self.start, self.split = n, units, start, split
        self.late = 1 if split else 0
        self.mid = n // 2
        self.terms, self.inward, self.across, self.back = bufs
        self.finish = finish
        (
            self.in_send,
            self.in_recv,
            self.cross_send,
            self.cross_recv,
            self.back_send0,
            self.back_recv0,
            self.back_send1,
            self.back_recv1,
            self.share_send,
        ) = sems
        self.credit = credit
        self.slots = self.inward.shape[0]
        self.done = start + (n + 1 if split else n - 1)
        me = lax.axis_index("col")
        self.side = lax.div(me, self.mid)
        self.hops = jnp.minimum(me, n - 1 - me)
        out = 2 * self.side - 1
        self.outer = jnp.clip(me + out, 0, n - 1)
        self.inner = me - out
        self.middle = self.hops == self.mid - 1

    def term(self, unit):
        return self.terms.at[lax.rem(unit, self.terms.shape[0])]

    def slot(self, unit):
        return self.inward.at[lax.rem(unit, self.slots)]

    def cross_slot(self, unit):
        return self.across.at[lax.rem(unit, self.across.shape[0])]

    def remote(self, src, dst, send, recv, to):
        return pltpu.make_async_remote_copy(
            src_ref=src,
            dst_ref=dst,
            send_sem=send,
            recv_sem=recv,
            device_id={"col": to},
            device_id_type=MESH,
        )

    def in_copy(self, unit, first):
        src = self.term(unit) if first else self.slot(unit)
        return self.remote(
            src, self.slot(unit), self.in_send.at[unit], self.in_recv.at[unit], self.inner
        )

    def cross_copy(self, unit):
        src = self.slot(unit).at[1 - self.side] if self.split else self.slot(unit)
        return self.remote(
            src,
            self.cross_slot(unit),
            self.cross_send.at[unit],
            self.cross_recv.at[unit],
            self.inner,
        )

    def result(self, unit, flow):
        if not self.split:
            return self.back.at[unit]
        return self.back.at[unit, self.side if flow == 0 else 1 - self.side]

    def back_copy(self, unit, flow):
        send, recv = (
            (self.back_send0, self.back_recv0) if flow == 0 else (self.back_send1, self.back_recv1)
        )
        ref = self.result(unit, flow)
        return self.remote(ref, ref, send.at[unit], recv.at[unit], self.outer)

    def share_copy(self, unit):
        ref = self.result(unit, 0)
        return self.remote(
            ref, ref, self.share_send.at[unit], self.back_recv1.at[unit], self.inner
        )

    def sums(self, tick):
        units, hops, middle = self.units, self.hops, self.middle
        unit = tick - self.start - hops
        sent = unit - 2

        @when_in(sent, units, middle)
        def _():
            self.cross_copy(sent).wait_send()

        @when_in(sent, units, hops == 0)
        def _():
            self.in_copy(sent, True).wait_send()

        if self.mid > 2:

            @when_in(sent, units, hops > 0, jnp.logical_not(middle))
            def _():
                self.in_copy(sent, False).wait_send()

        @when_in(sent, units, hops > 0, sent + self.slots < units)
        def _():
            pl.semaphore_signal(
                self.credit, inc=1, device_id={"col": self.outer}, device_id_type=MESH
            )

        @when_in(unit, units, hops > 0)
        def _():
            self.in_copy(unit, False).wait_recv()
            slot = self.slot(unit)
            slot[...] = (slot[...].astype(F32) + self.term(unit)[...].astype(F32)).astype(BF16)

        @when_in(unit, units, jnp.logical_not(middle), unit >= self.slots)
        def _():
            pl.semaphore_wait(self.credit, 1)

        @when_in(unit, units, hops == 0)
        def _():
            self.in_copy(unit, True).start()

        if self.mid > 2:

            @when_in(unit, units, hops > 0, jnp.logical_not(middle))
            def _():
                self.in_copy(unit, False).start()

        @when_in(unit, units, middle)
        def _():
            self.cross_copy(unit).start()

        ready = tick - self.start - self.mid

        @when_in(ready, units, middle)
        def _():
            self.cross_copy(ready).wait_recv()
            slot = self.slot(ready).at[self.side] if self.split else self.slot(ready)
            self.finish(self.side, ready, slot, self.cross_slot(ready), self.result(ready, 0))

        leaving = ready - self.late

        @when_in(leaving, units, middle)
        def _():
            self.back_copy(leaving, 0).start()
            if self.split:
                self.share_copy(leaving).start()

    def backs(self, tick):
        away = self.mid - 1 - self.hops
        unit0 = tick - self.start - self.mid - self.late - away

        @when_in(unit0, self.units, away > 0)
        def _():
            self.back_copy(unit0, 0).wait_recv()

        if self.mid > 2:

            @when_in(unit0, self.units, away > 0, self.hops > 0)
            def _():
                self.back_copy(unit0, 0).start()

        if self.split:
            unit1 = unit0 - 1

            @when_in(unit1, self.units)
            def _():
                self.back_copy(unit1, 1).wait_recv()

            @when_in(unit1, self.units, self.hops > 0)
            def _():
                self.back_copy(unit1, 1).start()

    def drain(self):
        @pl.loop(0, self.units)
        def _(unit):
            @pl.when(self.hops > 0)
            def _():
                self.back_copy(unit, 0).wait_send()
                if self.split:
                    self.back_copy(unit, 1).wait_send()

            if self.split:

                @pl.when(self.middle)
                def _():
                    self.share_copy(unit).wait_send()


class RowSum:
    def __init__(self, chips, units, start, buf, core_in, chip_in, sems, finish):
        self.chips, self.units, self.start = chips, units, start
        self.buf, self.core_in, self.chip_in = buf, core_in, chip_in
        self.finish = finish
        self.s1, self.r1, self.s2, self.r2 = sems
        self.done = start + 2
        row = lax.axis_index("row")
        self.core = lax.rem(row, 2)
        self.chip = lax.div(row, 2)
        self.partner = self.chip * 2 + 1 - self.core

    def first(self, unit):
        return pltpu.make_async_remote_copy(
            src_ref=self.buf.at[unit],
            dst_ref=self.core_in.at[lax.rem(unit, ROW_SLOTS)],
            send_sem=self.s1.at[unit],
            recv_sem=self.r1.at[unit],
            device_id={"row": self.partner},
            device_id_type=MESH,
        )

    def second(self, unit, step, core, arriving=False):
        half = core if arriving else self.core
        return pltpu.make_async_remote_copy(
            src_ref=self.buf.at[unit, half],
            dst_ref=self.chip_in.at[lax.rem(unit, ROW_SLOTS), step - 1, half],
            send_sem=self.s2.at[unit, step - 1, core],
            recv_sem=self.r2.at[unit, step - 1, half],
            device_id={"row": lax.rem(self.chip + step, self.chips) * 2 + core},
            device_id_type=MESH,
        )

    def begin(self, tick):
        unit = tick - self.start

        @when_in(unit, self.units)
        def _():
            self.first(unit).start()

    def steps(self, tick):
        others = [(step, core) for step in range(1, self.chips) for core in range(2)]
        unit2 = tick - self.start - 2

        @when_in(unit2, self.units)
        def _():
            for step, core in others:
                self.second(unit2, step, core, True).wait_recv()
            for step, core in others:
                self.second(unit2, step, core).wait_send()
            total = self.buf[unit2].astype(F32)
            for step in range(1, self.chips):
                total = total + self.chip_in[lax.rem(unit2, ROW_SLOTS), step - 1].astype(F32)
            self.buf[unit2] = self.finish(total)

        unit1 = tick - self.start - 1

        @when_in(unit1, self.units)
        def _():
            self.first(unit1).wait_recv()
            self.first(unit1).wait_send()
            self.buf[unit1] = (
                self.buf[unit1].astype(F32) + self.core_in[lax.rem(unit1, ROW_SLOTS)].astype(F32)
            ).astype(BF16)
            for step, core in others:
                self.second(unit1, step, core).start()


class Shares:
    def __init__(self, n, buf, sems):
        self.n, self.buf = n, buf
        self.send, self.recv = sems

    def copy(self, unit, step, arriving=False):
        me = lax.axis_index("col")
        slot = lax.rem(me + self.n - step, self.n) if arriving else me
        return pltpu.make_async_remote_copy(
            src_ref=self.buf.at[unit, slot],
            dst_ref=self.buf.at[unit, slot],
            send_sem=self.send.at[unit, step - 1],
            recv_sem=self.recv.at[unit, step - 1],
            device_id={"col": lax.rem(me + step, self.n)},
            device_id_type=MESH,
        )

    def put(self, unit, column):
        me = lax.axis_index("col")
        self.buf[unit, me] = jnp.broadcast_to(column, self.buf.shape[2:])
        for step in range(1, self.n):
            self.copy(unit, step).start()

    def wait(self, unit):
        for step in range(1, self.n):
            self.copy(unit, step, True).wait_recv()
            self.copy(unit, step).wait_send()

    def total(self, unit, rows=slice(None)):
        total = self.buf[unit, 0, rows]
        for index in range(1, self.n):
            total = total + self.buf[unit, index, rows]
        return total[:, :1]


def chain_kernel(
    n,
    chips,
    units,
    seq_ref,
    up_bias_ref,
    down_bias_ref,
    gain_ref,
    cot_ref,
    up_hbm,
    down_hbm,
    wg_hbm,
    wu_hbm,
    hidden_hbm,
    grad_merged_hbm,
    grad_pre_hbm,
    down_bias_grad,
    up_bias_grad,
    w_up_v,
    w_down_v,
    wg_v,
    wu_v,
    b_terms,
    b_in,
    b_cross,
    b_back,
    pre_act,
    c_buf,
    c_core,
    c_chip,
    squares,
    d_terms,
    d_in,
    d_cross,
    d_back,
    gate_kept,
    e_buf,
    e_core,
    e_chip,
    inners,
    f_terms,
    f_in,
    f_cross,
    f_back,
    w_sems,
    b_sems,
    d_sems,
    f_sems,
    credits,
    c_sem1,
    c_sem2,
    e_sem1,
    e_sem2,
    sq_sems,
    in_sems,
    out_sems,
):
    me = lax.axis_index("col")
    row = lax.axis_index("row")
    core = lax.rem(row, 2)
    chip = lax.div(row, 2)
    m = HALF
    rows = 2 * m

    loads = [
        pltpu.make_async_copy(src, dst, w_sems.at[k])
        for k, (src, dst) in enumerate(
            [(up_hbm, w_up_v), (down_hbm, w_down_v), (wg_hbm, wg_v), (wu_hbm, wu_v)]
        )
    ]
    for load in loads:
        load.start()
    down_bias_grad[...] = jnp.zeros_like(down_bias_grad)
    up_bias_grad[...] = jnp.zeros_like(up_bias_grad)

    barrier = pltpu.get_barrier_semaphore()
    for step in range(1, n):
        pl.semaphore_signal(
            barrier, inc=1, device_id={"col": lax.rem(me + step, n)}, device_id_type=MESH
        )
    pl.semaphore_signal(
        barrier, inc=1, device_id={"row": chip * 2 + 1 - core}, device_id_type=MESH
    )
    for step in range(1, chips):
        for to_core in range(2):
            pl.semaphore_signal(
                barrier,
                inc=1,
                device_id={"row": lax.rem(chip + step, chips) * 2 + to_core},
                device_id_type=MESH,
            )
    pl.semaphore_wait(barrier, n - 1 + 1 + 2 * (chips - 1))

    def gelu_finish(half, unit, ours, theirs, out):
        value = ours[:, 0].astype(F32) + theirs[:, 0].astype(F32) + up_bias_ref[...]
        pre_act[unit] = value
        out[:, 0] = (0.5 * value * (1.0 + lax.erf(value / math.sqrt(2.0)))).astype(BF16)

    def swiglu_finish(half, step, ours, theirs, out):
        unit = lax.div(step, 2)
        mine = pl.ds(pl.multiple_of(half * m, m), m)
        inv = lax.rsqrt(squares_io.total(unit, mine) / D + EPS_NORM)
        value = ((ours[...].astype(F32) + theirs[...].astype(F32)) * inv).astype(BF16).astype(F32)

        @pl.when(lax.rem(step, 2) == 0)
        def _():
            gate_kept[...] = value

        @pl.when(lax.rem(step, 2) == 1)
        def _():
            gate = gate_kept[...]
            logistic = 1.0 / (1.0 + jnp.exp(-gate))
            through = cot_ref[unit].astype(F32) * logistic
            d_back[step - 1, half] = (through * value * (1.0 + gate * (1.0 - logistic))).astype(
                BF16
            )
            out[...] = (through * gate).astype(BF16)

    def slope_finish(half, unit, ours, theirs, out):
        value = ours[:, 0].astype(F32) + theirs[:, 0].astype(F32)
        out[:, 0] = (value * gelu_slope(pre_act[unit])).astype(BF16)

    def parts(sems, count):
        return [sems.at[k] for k in range(count)]

    squares_io = Shares(n, squares, parts(sq_sems, 2))
    inners_io = Shares(n, inners, parts(in_sems, 2))
    line_b = Line(
        n,
        units,
        0,
        False,
        (b_terms, b_in, b_cross, b_back),
        parts(b_sems, 9),
        credits.at[0],
        gelu_finish,
    )
    sum_c = RowSum(
        chips,
        units,
        line_b.done,
        c_buf,
        c_core,
        c_chip,
        parts(c_sem1, 2) + parts(c_sem2, 2),
        lambda total: (total + down_bias_ref[...]).astype(BF16),
    )
    d_start = sum_c.done + 2
    d_done = d_start + n // 2 + 1
    line_d = Line(
        n,
        2 * units,
        2 * d_start,
        True,
        (d_terms, d_in, d_cross, d_back),
        parts(d_sems, 9),
        credits.at[1],
        swiglu_finish,
    )
    sum_e = RowSum(
        chips,
        units,
        d_done + 2,
        e_buf,
        e_core,
        e_chip,
        parts(e_sem1, 2) + parts(e_sem2, 2),
        lambda total: total.astype(BF16),
    )
    line_f = Line(
        n,
        units,
        sum_e.done + 1,
        False,
        (f_terms, f_in, f_cross, f_back),
        parts(f_sems, 9),
        credits.at[2],
        slope_finish,
    )
    ticks = units + line_f.done + 1

    def out_copies(unit):
        return [
            pltpu.make_async_copy(src.at[unit], dst.at[unit], out_sems.at[k, unit])
            for k, (src, dst) in enumerate(
                [(b_back, hidden_hbm), (e_buf, grad_merged_hbm), (f_back, grad_pre_hbm)]
            )
        ]

    def tick_body(tick, carry):
        unit_q = tick - (sum_c.done + 1)

        @when_in(unit_q, units)
        def _():
            squares_io.wait(unit_q)

        line_d.sums(2 * tick)
        line_d.backs(2 * tick)

        unit_f = tick - line_f.start

        @when_in(unit_f, units)
        def _():
            inners_io.wait(unit_f)
            inv = lax.rsqrt(squares_io.total(unit_f) / D + EPS_NORM)
            factor = inv * inv * inv / D * inners_io.total(unit_f)
            merged = c_buf[unit_f].reshape(rows, -1).astype(F32)
            gained = e_buf[unit_f].reshape(rows, -1).astype(F32) * gain_ref[...]
            grad = (inv * gained - merged * factor).astype(BF16)
            e_buf[unit_f] = grad.reshape(2, m, -1)
            out_copies(unit_f)[1].start()
            down_bias_grad[...] += jnp.sum(grad.astype(F32), axis=0, keepdims=True)
            slot = lax.rem(unit_f, f_terms.shape[0])
            for at, size in tiles_of(w_down_v.shape[0], 640):
                part = dot_cols(grad, w_down_v[pl.ds(at, size), :]).astype(BF16)
                f_terms[slot, :, 0, :, pl.ds(at, size)] = part.reshape(2, m, size)

        line_f.sums(tick)
        line_f.backs(tick)

        unit_z = tick - line_f.done

        @when_in(unit_z, units)
        def _():
            out_copies(unit_z)[2].start()
            grad_pre = f_back[unit_z, :, 0].reshape(rows, -1)
            up_bias_grad[...] += jnp.sum(grad_pre.astype(F32), axis=0, keepdims=True)

        sum_e.steps(tick)
        unit_i = tick - sum_e.done

        @when_in(unit_i, units)
        def _():
            merged = c_buf[unit_i].reshape(rows, -1).astype(F32)
            gained = e_buf[unit_i].reshape(rows, -1).astype(F32) * gain_ref[...]
            inners_io.put(unit_i, jnp.sum(merged * gained, axis=1, keepdims=True))

        def backward(unit, count, first):
            steps = pl.ds(2 * unit, 2 * count)
            grads = d_back[steps].reshape(count, 2, 2, m, -1)
            grad_gate = grads[:, 0].reshape(count * rows, -1)
            grad_up = grads[:, 1].reshape(count * rows, -1)
            tiles = tiles_of(wg_v.shape[1], 512)
            near = (len(tiles) + 1) // 2
            for at, size in tiles[:near] if first else tiles[near:]:
                part = (
                    dot_rows(grad_gate, wg_v[:, pl.ds(at, size)])
                    + dot_rows(grad_up, wu_v[:, pl.ds(at, size)])
                ).astype(BF16)
                e_buf[pl.ds(unit, count), :, :, pl.ds(at, size)] = part.reshape(count, 2, m, size)

        def forward(unit, count, first):
            merged = c_buf[pl.ds(unit, count)].reshape(count * rows, -1).astype(F32)
            lifted = (merged * gain_ref[...]).astype(BF16)
            plane, weight = (0, wg_v) if first else (1, wu_v)
            slots = [lax.rem(2 * (unit + k), d_terms.shape[0]) + plane for k in range(count)]
            for at, size in tiles_of(weight.shape[0], 1024):
                part = dot_cols(lifted, weight[pl.ds(at, size), :]).astype(BF16)
                part = part.reshape(count, 2, m, size)
                for k in range(count):
                    d_terms[slots[k], :, :, pl.ds(at, size)] = part[k]

        def by_pairs(unit, work, first):
            @when_in(unit, units - 1, lax.rem(unit, 2) == 0)
            def _():
                work(unit, 2, first)

            if units % 2:

                @pl.when(unit == units - 1)
                def _():
                    work(unit, 1, first)

        @pl.when(tick == d_start - 1)
        def _():
            loads[2].wait()
            loads[3].wait()

        by_pairs(tick - d_done - 2, backward, False)
        sum_e.begin(tick)
        by_pairs(tick - d_start, forward, False)

        line_d.sums(2 * tick + 1)
        line_d.backs(2 * tick + 1)

        sum_c.steps(tick)

        unit_s = tick - sum_c.done

        @when_in(unit_s, units)
        def _():
            merged = c_buf[unit_s].reshape(rows, -1).astype(F32)
            squares_io.put(unit_s, jnp.sum(merged * merged, axis=1, keepdims=True))

        @pl.when(tick == 0)
        def _():
            loads[0].wait()

        unit_b = tick

        @when_in(unit_b, units)
        def _():
            slot = lax.rem(unit_b, b_terms.shape[0])
            seq = seq_ref[unit_b].reshape(rows, -1)
            for at, size in tiles_of(w_up_v.shape[1], 640):
                part = dot_rows(seq, w_up_v[:, pl.ds(at, size)]).astype(BF16)
                b_terms[slot, :, 0, :, pl.ds(at, size)] = part.reshape(2, m, size)

        line_b.sums(tick)
        line_b.backs(tick)

        @pl.when(tick == sum_c.start)
        def _():
            loads[1].wait()

        unit_c = tick - sum_c.start

        @when_in(unit_c, units)
        def _():
            out_copies(unit_c)[0].start()
            hidden = b_back[unit_c, :, 0].reshape(rows, -1)
            for at, size in tiles_of(w_down_v.shape[1], 512):
                part = dot_rows(hidden, w_down_v[:, pl.ds(at, size)]).astype(BF16)
                c_buf[unit_c, :, :, pl.ds(at, size)] = part.reshape(2, m, size)

        sum_c.begin(tick)

        by_pairs(tick - d_done - 1, backward, True)
        by_pairs(tick - (d_start - 1), forward, True)

        return carry

    lax.fori_loop(0, ticks, tick_body, 0)
    line_b.drain()
    line_d.drain()
    line_f.drain()

    @pl.loop(0, units)
    def _(unit):
        for copy in out_copies(unit):
            copy.wait()


def chain(units, branch_id, seq, cot, rows_of, operands):
    merger_up, merger_down, w_gate, w_up = operands
    n = lax.axis_size("col")
    chips = lax.axis_size("row") // 2
    m = HALF
    mdim, hid = merger_up.shape
    width = merger_down.shape[1]
    ffw = w_gate.shape[1]
    vmem = pl.BlockSpec(memory_space=pltpu.VMEM)
    hbm = pl.BlockSpec(memory_space=pltpu.HBM)
    dma = pltpu.SemaphoreType.DMA
    term_slots = max(SLOTS, n // 2 + 2)
    flops = 2 * units * 2 * m * (mdim * hid + 2 * hid * width + 4 * width * ffw)
    return pl.pallas_call(
        functools.partial(chain_kernel, n, chips, units),
        out_shape=[
            jax.ShapeDtypeStruct((units, 2, 1, m, hid), BF16),
            jax.ShapeDtypeStruct((units, 2, m, width), BF16),
            jax.ShapeDtypeStruct((units, 2, 1, m, hid), BF16),
            jax.ShapeDtypeStruct((1, width), F32),
            jax.ShapeDtypeStruct((1, hid), F32),
        ],
        in_specs=[vmem] * 5 + [hbm] * 4,
        out_specs=[hbm] * 3 + [vmem] * 2,
        scratch_shapes=[
            pltpu.VMEM(merger_up.shape, BF16),
            pltpu.VMEM(merger_down.shape, BF16),
            pltpu.VMEM((ffw, width), BF16),
            pltpu.VMEM((ffw, width), BF16),
            pltpu.VMEM((term_slots, 2, 1, m, hid), BF16),
            pltpu.VMEM((SLOTS, 2, 1, m, hid), BF16),
            pltpu.VMEM((SLOTS, 2, 1, m, hid), BF16),
            pltpu.VMEM((units, 2, 1, m, hid), BF16),
            pltpu.VMEM((units, 2, m, hid), F32),
            pltpu.VMEM((units, 2, m, width), BF16),
            pltpu.VMEM((ROW_SLOTS, 2, m, width), BF16),
            pltpu.VMEM((ROW_SLOTS, chips - 1, 2, m, width), BF16),
            pltpu.VMEM((units, n, 2 * m, 128), F32),
            pltpu.VMEM((2 * term_slots, 2, m, ffw), BF16),
            pltpu.VMEM((SLOTS + 2, 2, m, ffw), BF16),
            pltpu.VMEM((SLOTS + 2, m, ffw), BF16),
            pltpu.VMEM((2 * units, 2, m, ffw), BF16),
            pltpu.VMEM((m, ffw), F32),
            pltpu.VMEM((units, 2, m, width), BF16),
            pltpu.VMEM((ROW_SLOTS, 2, m, width), BF16),
            pltpu.VMEM((ROW_SLOTS, chips - 1, 2, m, width), BF16),
            pltpu.VMEM((units, n, 2 * m, 128), F32),
            pltpu.VMEM((term_slots, 2, 1, m, hid), BF16),
            pltpu.VMEM((SLOTS, 2, 1, m, hid), BF16),
            pltpu.VMEM((SLOTS, 2, 1, m, hid), BF16),
            pltpu.VMEM((units, 2, 1, m, hid), BF16),
            dma((4,)),
            dma((9, units)),
            dma((9, 2 * units)),
            dma((9, units)),
            pltpu.SemaphoreType.REGULAR((3,)),
            dma((2, units)),
            dma((2, units, chips - 1, 2)),
            dma((2, units)),
            dma((2, units, chips - 1, 2)),
            dma((2, units, n - 1)),
            dma((2, units, n - 1)),
            dma((3, units)),
        ],
        cost_estimate=pl.CostEstimate(
            flops=flops, bytes_accessed=2 * (mdim * hid + hid * width + 2 * width * ffw),
            transcendentals=units * m * ffw,
        ),
        compiler_params=pltpu.CompilerParams(
            collective_id=branch_id, has_side_effects=True, vmem_limit_bytes=63 * 1024 * 1024
        ),
    )(
        seq,
        *rows_of,
        cot,
        merger_up,
        merger_down,
        w_gate.T,
        w_up.T,
    )


def half_counts(placement, patch_counts, n_col):
    images = placement.shape[0]
    fill = patch_counts // 4
    col = placement // (images // n_col)

    def among(chosen):
        return jnp.sum(jnp.where(chosen, fill, 0))

    mid = n_col // 2
    return among(col < mid), among(col >= mid), among(col == mid - 1), among(col == mid)


def half_plan(placement, patch_counts, tokens, n_col, cap):
    images = placement.shape[0]
    ids = jnp.arange(images, dtype=jnp.int32)
    hit = placement[:, None] == ids[None, :]
    fill = jnp.sum(jnp.where(hit, (patch_counts // 4)[:, None], 0), axis=0)
    half = ids // (images // 2)
    count0 = jnp.sum(jnp.where(half == 0, fill, 0))
    count1 = jnp.sum(jnp.where(half == 1, fill, 0))
    start = jnp.sum(jnp.where(ids[None, :] < ids[:, None], fill[None, :], 0), axis=1)
    place = jnp.arange(BLK, dtype=jnp.int32)
    order = start[:, None] + place[None, :]
    half = half[:, None]
    rank = jnp.where(half == 0, order, count0 + count1 - 1 - order)
    over = rank >= cap
    rank = jnp.where(over, jnp.where(half == 0, count1, count0) + rank - cap, rank)
    half = jnp.where(over, 1 - half, half)
    real = place[None, :] < fill[:, None]
    slot = (rank // HALF) * (2 * HALF) + half * HALF + rank % HALF
    slot = jnp.where(real, slot, -1)
    kept = jnp.where(real & jnp.logical_not(over), rank, -1).reshape(n_col, -1)
    spilled = jnp.where(real & over, rank - jnp.where(half == 0, count0, count1), -1)
    counts = (count0, count1)
    over_counts = [jnp.maximum(count - cap, 0) for count in counts]
    by_image = jnp.sum(jnp.where(hit[:, :, None], slot[None, :, :], 0), axis=1)
    return kept, spilled.reshape(n_col, -1), counts, over_counts, by_image


def half_step(units, branch_id, sequence_in, plan, operands):
    arrival, near, rows_of, cot_near = plan
    merger_up, merger_down, w_gate, w_up = operands[0], operands[2], operands[5], operands[6]
    packed = units * 2 * HALF
    sequence = pick(one_hot(arrival, 0, packed), sequence_in).astype(BF16)
    cot = pick(one_hot(near, 0, units * HALF), cot_near).astype(BF16)
    hidden_all, grad_merged_all, grad_pre_all, down_bias_grad, up_bias_grad = chain(
        units,
        branch_id,
        sequence.reshape(units, 2, HALF, -1),
        cot.reshape(units, HALF, -1),
        rows_of,
        (merger_up, merger_down, w_gate, w_up),
    )
    hidden_all = hidden_all.reshape(packed, -1)
    grad_merged_all = grad_merged_all.reshape(packed, -1)
    grad_pre_all = grad_pre_all.reshape(packed, -1)
    merger_down_grad = lax.dot_general(
        hidden_all, grad_merged_all, CONTRACT_ROWS, preferred_element_type=F32
    )
    merger_up_grad = lax.dot_general(
        sequence, grad_pre_all, CONTRACT_ROWS, preferred_element_type=F32
    )
    return (merger_up_grad, up_bias_grad[0], merger_down_grad, down_bias_grad[0])


def shards(
    patches,
    patch_gain,
    patch_bias,
    merger_up,
    merger_up_bias,
    merger_down,
    merger_down_bias,
    norm_gain,
    w_gate,
    w_up,
    hidden_cotangent,
    placement,
    patch_counts,
):
    n_col = lax.axis_size("col")
    held = hidden_cotangent.shape[0]
    left, right, left_near, right_near = half_counts(placement, patch_counts, n_col)
    own_rows = jnp.maximum(
        (left + right + 1) // 2,
        jnp.maximum(
            left - jnp.minimum(left_near, SPILL), right - jnp.minimum(right_near, SPILL)
        ),
    )
    real_rows = own_rows
    for step in range(1, lax.axis_size("group")):
        real_rows = jnp.maximum(real_rows, shift_by(own_rows, "group", step))
    most = held * n_col // 2 // HALF
    counts = [most * sixteenths // 16 for sixteenths in SIXTEENTHS]
    branch = sum((real_rows > units * HALF).astype(jnp.int32) for units in counts)
    image_tokens = patch_tokens(patches, patch_gain, patch_bias)
    slot_count = image_tokens.shape[1]
    feat_width = image_tokens.shape[2] // n_col
    sending = image_tokens.reshape(IMG_ROW * slot_count, n_col, feat_width)
    sending = jnp.transpose(sending, (1, 0, 2))
    col_index = lax.axis_index("col")
    pieces = [lax.dynamic_index_in_dim(sending, col_index, keepdims=False)]
    for step in range(1, n_col):
        outgoing = lax.dynamic_index_in_dim(
            sending, (col_index + step) % n_col, keepdims=False
        )
        pieces.append(shift_by(outgoing, "col", step))
    pieces[0], late_cot, late_placement, late_counts = lax.optimization_barrier(
        (pieces[0], hidden_cotangent, placement, patch_counts)
    )
    mid = n_col // 2
    limit = jnp.asarray(counts, jnp.int32)[jnp.minimum(branch, len(counts) - 1)] * HALF
    n_row = lax.axis_size("row")
    kept, spilled, in_half, over, by_image = half_plan(
        late_placement, late_counts, held * n_col, n_col, limit
    )
    arrival = by_image.reshape(n_row, IMG_ROW, n_col, BLK // n_col)
    arrival = jnp.stack(
        [
            lax.dynamic_index_in_dim(arrival, (col_index - step) % n_col, axis=2, keepdims=False)
            for step in range(n_col)
        ],
        axis=1,
    ).reshape(-1)
    cot_near = [late_cot]
    for step in range(1, mid):
        cot_near.append(
            lax.ppermute(late_cot, "col", [(mid - 1 - step, mid - 1), (mid + step, mid)])
        )
    spilled_here = lax.dynamic_index_in_dim(spilled, col_index, keepdims=False)
    spilling = pick(one_hot(spilled_here, 0, SPILL), late_cot).astype(BF16)
    cot_near.append(lax.ppermute(spilling, "col", [(mid - 1, mid), (mid, mid - 1)]))
    cot_near = jnp.concatenate(cot_near, axis=0)
    turn = jnp.arange(SPILL, dtype=jnp.int32)
    right_side = col_index >= mid
    came = jnp.where(right_side, over[0], over[1])
    came_rank = jnp.where(turn < came, turn + jnp.where(right_side, in_half[1], in_half[0]), -1)
    near = jnp.concatenate(
        [jnp.where(right_side, kept[mid:], kept[:mid][::-1]).reshape(-1), came_rank]
    )
    merged = jnp.concatenate(pieces, axis=0)
    gathered_in = lax.all_gather(merged, "row", axis=0, tiled=True)
    operands = (
        merger_up,
        merger_up_bias,
        merger_down,
        merger_down_bias,
        norm_gain,
        w_gate,
        w_up,
        hidden_cotangent,
        placement,
        patch_counts,
    )
    steps = [
        functools.partial(half_step, units, number) for number, units in enumerate(counts)
    ]

    rows_of = tuple(
        vector.astype(F32)[None] for vector in (merger_up_bias, merger_down_bias, norm_gain)
    )

    def whole_step(sequence_in, plan, operands):
        return packed_step(held, sequence_in, operands)

    plan = (arrival, near, rows_of, cot_near)
    return lax.switch(branch, steps + [whole_step], gathered_in, plan, operands)


def solution(mesh):
    in_specs = (
        P(("group", "row"), "col", None),
        P(),
        P(),
        P("col", "row"),
        P("row"),
        P("row", "col"),
        P("col"),
        P("col"),
        P("col", "row"),
        P("col", "row"),
        P(("group", "col"), "row"),
        P("group"),
        P("group"),
    )
    out_specs = (
        P(("group", "col"), "row"),
        P(("group", "row")),
        P(("group", "row"), "col"),
        P(("group", "col")),
    )
    return jax.shard_map(shards, mesh=mesh, in_specs=in_specs, out_specs=out_specs, check_vma=False)
```

```python
import functools
import math

import jax
import jax.numpy as jnp
from jax import lax
from jax.experimental import pallas as pl
from jax.experimental.pallas import tpu as pltpu
from jax.sharding import PartitionSpec as P

D = 8192
BLK = 16
IMG_ROW = 8


EPS_PATCH = 1e-06
EPS_NORM = 1e-06
CONTRACT_ROWS = (((0,), (0,)), ((), ()))
CONTRACT_COLS = (((1,), (1,)), ((), ()))


def gelu_slope(inputs):
    cumulative = 0.5 * (1.0 + jax.scipy.special.erf(inputs / math.sqrt(2.0)))
    return cumulative + inputs * jnp.exp(-0.5 * inputs * inputs) / math.sqrt(2.0 * math.pi)


def patch_tokens(patches, patch_gain, patch_bias):
    values = patches.astype(jnp.float32)
    center = values - jnp.mean(values, axis=-1, keepdims=True)
    spread = jnp.mean(center * center, axis=-1, keepdims=True)
    normed = center * lax.rsqrt(spread + EPS_PATCH) * patch_gain.astype(
        jnp.float32
    ) + patch_bias.astype(jnp.float32)
    image_count, patch_slots, patch_width = patches.shape
    return normed.astype(jnp.bfloat16).reshape(image_count, patch_slots // 4, 4 * patch_width)


def swiglu_grads(gate_out, up_out, cotangent):
    gate_f = gate_out.astype(jnp.float32)
    up_f = up_out.astype(jnp.float32)
    masked = cotangent.astype(jnp.float32)
    logistic = jax.nn.sigmoid(gate_f)
    grad_gate = (masked * up_f * logistic * (1.0 + gate_f * (1.0 - logistic))).astype(jnp.bfloat16)
    grad_up = (masked * gate_f * logistic).astype(jnp.bfloat16)
    return (grad_gate, grad_up)


def pack_plan(placement, patch_counts, tokens, n_row, n_col, cap):
    images = placement.shape[0]
    rows = tokens // n_col
    blocks = rows // BLK
    ids = jnp.arange(images, dtype=jnp.int32)
    cols = jnp.arange(n_col, dtype=jnp.int32)
    hit = placement[:, None] == ids[None, :]
    fill = jnp.sum(jnp.where(hit, (patch_counts // 4)[:, None], 0), axis=0)
    owner = ids // blocks
    before = (owner[:, None] == owner[None, :]) & (ids[None, :] < ids[:, None])
    start = jnp.sum(jnp.where(before, fill[None, :], 0), axis=1)
    count = jnp.sum(jnp.where(owner[None, :] == cols[:, None], fill[None, :], 0), axis=1)
    over = jnp.maximum(count - cap, 0)
    free = jnp.maximum(cap - count, 0)
    lower = cols[None, :] < cols[:, None]
    over_start = jnp.sum(jnp.where(lower, over[None, :], 0), axis=1)
    free_start = jnp.sum(jnp.where(lower, free[None, :], 0), axis=1)

    def spill_slot(number):
        inside = (number[..., None] >= free_start) & (number[..., None] < free_start + free)
        return jnp.sum(
            jnp.where(inside, cols * cap + count + number[..., None] - free_start, 0), axis=-1
        )

    place = jnp.arange(BLK, dtype=jnp.int32)
    rank = start[:, None] + place[None, :]
    real = place[None, :] < fill[:, None]
    owner_over = jnp.sum(jnp.where(owner[:, None] == cols[None, :], over_start[None, :], 0), axis=1)
    slot = jnp.where(
        rank < cap,
        owner[:, None] * cap + rank,
        spill_slot(owner_over[:, None] + rank - cap),
    )
    slot = jnp.where(real, slot, -1)
    rank = jnp.where(real, rank, -1)
    by_image = jnp.sum(jnp.where(hit[:, :, None], slot[None, :, :], 0), axis=1)
    extra = jnp.arange(rows - cap, dtype=jnp.int32)
    extra_slot = jnp.where(
        extra[None, :] < over[:, None], spill_slot(over_start[:, None] + extra[None, :]), -1
    )
    return slot.reshape(-1), rank.reshape(-1), by_image, extra_slot.reshape(-1)


def one_hot(slots, first, size):
    return (slots[None, :] - first == jnp.arange(size, dtype=jnp.int32)[:, None]).astype(
        jnp.bfloat16
    )


def pick(selection, values):
    return jnp.dot(selection, values, preferred_element_type=jnp.float32)


def shift_by(values, axis, step):
    size = lax.axis_size(axis)
    return lax.ppermute(values, axis, [(i, (i + step) % size) for i in range(size)])


def sum_direct(part, axis):
    total = part
    for step in range(1, lax.axis_size(axis)):
        total = total + shift_by(part, axis, step)
    return total


def gather_small(part, axis):
    size = lax.axis_size(axis)
    index = lax.axis_index(axis)
    ids = jnp.arange(size, dtype=jnp.int32)[:, None]
    out = jnp.where(ids == index, part[None, :], 0.0)
    for step in range(1, size):
        came = shift_by(part, axis, step)
        out = jnp.where(ids == (index - step) % size, came[None, :], out)
    return out.reshape(-1)


def scatter_direct(partial, axis):
    size = lax.axis_size(axis)
    index = lax.axis_index(axis)
    rows = partial.shape[0] // size

    def piece(owner):
        return lax.dynamic_slice_in_dim(partial, owner * rows, rows)

    total = piece(index).astype(jnp.float32)
    for step in range(1, size):
        came = shift_by(piece((index + step) % size), axis, step)
        total = total + came.astype(jnp.float32)
    return total


def packed_step(cap, sequence_in, operands):
    (
        merger_up,
        merger_up_bias,
        merger_down,
        merger_down_bias,
        norm_gain,
        w_gate,
        w_up,
        hidden_cotangent,
        placement,
        patch_counts,
    ) = operands
    n_row = lax.axis_size("row")
    n_col = lax.axis_size("col")
    col_index = lax.axis_index("col")
    tokens = sequence_in.shape[0]
    held = hidden_cotangent.shape[0]
    packed = cap * n_col
    slot, rank, by_image, extra_slot = pack_plan(
        placement, patch_counts, tokens, n_row, n_col, cap
    )
    arrival = by_image.reshape(n_row, IMG_ROW, n_col, BLK // n_col)
    arrival = jnp.stack(
        [
            lax.dynamic_index_in_dim(arrival, (col_index - step) % n_col, axis=2, keepdims=False)
            for step in range(n_col)
        ],
        axis=1,
    ).reshape(-1)
    sequence = pick(one_hot(arrival, 0, packed), sequence_in).astype(jnp.bfloat16)
    slot_here = lax.dynamic_slice_in_dim(slot, col_index * held, held)
    cotangent = pick(one_hot(slot_here, col_index * cap, cap), hidden_cotangent)
    if cap < held:
        rank_here = lax.dynamic_slice_in_dim(rank, col_index * held, held)
        spilled = pick(one_hot(rank_here, cap, held - cap), hidden_cotangent).astype(jnp.bfloat16)
        spilled_all = lax.all_gather(spilled, "col", axis=0, tiled=True)
        cotangent = cotangent + pick(one_hot(extra_slot, col_index * cap, cap), spilled_all)
    cotangent = cotangent.astype(jnp.bfloat16)

    pre_act = lax.psum_scatter(
        pick(sequence, merger_up).astype(jnp.bfloat16), "col", scatter_dimension=0, tiled=True
    ).astype(jnp.float32) + merger_up_bias.astype(jnp.float32)
    hidden_one = jax.nn.gelu(pre_act, approximate=False).astype(jnp.bfloat16)
    hidden_all = lax.all_gather(hidden_one, "col", axis=0, tiled=True)
    merged_out = lax.optimization_barrier(
        (
            scatter_direct(pick(hidden_all, merger_down).astype(jnp.bfloat16), "row")
            + merger_down_bias.astype(jnp.float32)
        ).astype(jnp.bfloat16)
    )

    def row_sums(part):
        return gather_small(sum_direct(part, "col"), "row")

    merged_f = merged_out.astype(jnp.float32)
    merged_all = lax.all_gather(merged_out, "row", axis=0, tiled=True).astype(jnp.float32)
    square_sums = row_sums(jnp.sum(merged_f * merged_f, axis=1))
    inv_rms = lax.rsqrt(square_sums / D + EPS_NORM)
    gain = norm_gain.astype(jnp.float32)
    normed_all = lax.optimization_barrier(
        (merged_all * inv_rms[:, None] * gain).astype(jnp.bfloat16)
    )

    def block_sums(rows, weight):
        return lax.psum_scatter(
            pick(rows, weight).astype(jnp.bfloat16), "col", scatter_dimension=0, tiled=True
        )

    gate_out = block_sums(normed_all, w_gate)
    up_out = block_sums(normed_all, w_up)
    grad_gate, grad_up = swiglu_grads(gate_out, up_out, cotangent)
    grad_gate_all = lax.all_gather(grad_gate, "col", axis=0, tiled=True)
    grad_up_all = lax.all_gather(grad_up, "col", axis=0, tiled=True)
    from_gate = lax.dot_general(
        grad_gate_all, w_gate, CONTRACT_COLS, preferred_element_type=jnp.float32
    )
    from_up = lax.dot_general(
        grad_up_all, w_up, CONTRACT_COLS, preferred_element_type=jnp.float32
    )
    grad_normed = scatter_direct((from_gate + from_up).astype(jnp.bfloat16), "row").astype(
        jnp.bfloat16
    )
    inner = row_sums(jnp.sum(merged_f * (gain * grad_normed.astype(jnp.float32)), axis=1))
    gained_all = gain * lax.all_gather(grad_normed, "row", axis=0, tiled=True).astype(jnp.float32)
    grad_merged_all = (
        inv_rms[:, None] * gained_all
        - merged_all * (inv_rms * inv_rms * inv_rms / D * inner)[:, None]
    ).astype(jnp.bfloat16)
    grad_hidden = lax.psum_scatter(
        lax.dot_general(
            grad_merged_all, merger_down, CONTRACT_COLS, preferred_element_type=jnp.float32
        ).astype(jnp.bfloat16),
        "col",
        scatter_dimension=0,
        tiled=True,
    ).astype(jnp.float32)
    merger_down_grad = lax.dot_general(
        hidden_all, grad_merged_all, CONTRACT_ROWS, preferred_element_type=jnp.float32
    )
    merger_down_bias_grad = jnp.sum(grad_merged_all, axis=0, dtype=jnp.float32)
    grad_pre = (grad_hidden * gelu_slope(pre_act)).astype(jnp.bfloat16)
    grad_pre_all = lax.all_gather(grad_pre, "col", axis=0, tiled=True)
    merger_up_grad = lax.dot_general(
        sequence, grad_pre_all, CONTRACT_ROWS, preferred_element_type=jnp.float32
    )
    merger_up_bias_grad = jnp.sum(grad_pre_all, axis=0, dtype=jnp.float32)
    return (merger_up_grad, merger_up_bias_grad, merger_down_grad, merger_down_bias_grad)


MESH = pl.DeviceIdType.MESH
F32 = jnp.float32
BF16 = jnp.bfloat16
HALF = 16
SLOTS = 4


def dot_rows(left, right):
    return jnp.dot(left, right, preferred_element_type=F32)


def dot_cols(left, right):
    return lax.dot_general(left, right, CONTRACT_COLS, preferred_element_type=F32)


def tiles_of(width, tile):
    return [(at, min(tile, width - at)) for at in range(0, width, tile)]


def when_in(unit, units, *more):
    ok = (unit >= 0) & (unit < units)
    for cond in more:
        ok = ok & cond
    return pl.when(ok)


class Line:
    def __init__(self, n, units, start, split, bufs, sems, credit, finish):
        self.n, self.units, self.start, self.split = n, units, start, split
        self.mid = n // 2
        self.terms, self.inward, self.across, self.back = bufs
        self.finish = finish
        (
            self.in_send,
            self.in_recv,
            self.cross_send,
            self.cross_recv,
            self.back_send0,
            self.back_recv0,
            self.back_send1,
            self.back_recv1,
            self.share_send,
        ) = sems
        self.credit = credit
        self.slots = self.inward.shape[0]
        self.done = start + (n if split else n - 1)
        me = lax.axis_index("col")
        self.side = lax.div(me, self.mid)
        self.hops = jnp.minimum(me, n - 1 - me)
        out = 2 * self.side - 1
        self.outer = jnp.clip(me + out, 0, n - 1)
        self.inner = me - out
        self.middle = self.hops == self.mid - 1

    def term(self, unit):
        return self.terms.at[lax.rem(unit, self.terms.shape[0])]

    def slot(self, unit):
        return self.inward.at[lax.rem(unit, self.slots)]

    def cross_slot(self, unit):
        return self.across.at[lax.rem(unit, self.across.shape[0])]

    def remote(self, src, dst, send, recv, to):
        return pltpu.make_async_remote_copy(
            src_ref=src,
            dst_ref=dst,
            send_sem=send,
            recv_sem=recv,
            device_id={"col": to},
            device_id_type=MESH,
        )

    def in_copy(self, unit, first):
        src = self.term(unit) if first else self.slot(unit)
        return self.remote(
            src, self.slot(unit), self.in_send.at[unit], self.in_recv.at[unit], self.inner
        )

    def cross_copy(self, unit):
        src = self.slot(unit).at[1 - self.side] if self.split else self.slot(unit)
        return self.remote(
            src,
            self.cross_slot(unit),
            self.cross_send.at[unit],
            self.cross_recv.at[unit],
            self.inner,
        )

    def result(self, unit, flow):
        if not self.split:
            return self.back.at[unit]
        return self.back.at[unit, self.side if flow == 0 else 1 - self.side]

    def back_copy(self, unit, flow):
        send, recv = (
            (self.back_send0, self.back_recv0) if flow == 0 else (self.back_send1, self.back_recv1)
        )
        ref = self.result(unit, flow)
        return self.remote(ref, ref, send.at[unit], recv.at[unit], self.outer)

    def share_copy(self, unit):
        ref = self.result(unit, 0)
        return self.remote(
            ref, ref, self.share_send.at[unit], self.back_recv1.at[unit], self.inner
        )

    def sums(self, tick):
        units, hops, middle = self.units, self.hops, self.middle
        unit = tick - self.start - hops
        sent = unit - 2

        @when_in(sent, units, middle)
        def _():
            self.cross_copy(sent).wait_send()

        @when_in(sent, units, hops == 0)
        def _():
            self.in_copy(sent, True).wait_send()

        if self.mid > 2:

            @when_in(sent, units, hops > 0, jnp.logical_not(middle))
            def _():
                self.in_copy(sent, False).wait_send()

        @when_in(sent, units, hops > 0, sent + self.slots < units)
        def _():
            pl.semaphore_signal(
                self.credit, inc=1, device_id={"col": self.outer}, device_id_type=MESH
            )

        @when_in(unit, units, hops > 0)
        def _():
            self.in_copy(unit, False).wait_recv()
            slot = self.slot(unit)
            slot[...] = (slot[...].astype(F32) + self.term(unit)[...].astype(F32)).astype(BF16)

        @when_in(unit, units, jnp.logical_not(middle), unit >= self.slots)
        def _():
            pl.semaphore_wait(self.credit, 1)

        @when_in(unit, units, hops == 0)
        def _():
            self.in_copy(unit, True).start()

        if self.mid > 2:

            @when_in(unit, units, hops > 0, jnp.logical_not(middle))
            def _():
                self.in_copy(unit, False).start()

        @when_in(unit, units, middle)
        def _():
            self.cross_copy(unit).start()

        ready = tick - self.start - self.mid

        @when_in(ready, units, middle)
        def _():
            self.cross_copy(ready).wait_recv()
            slot = self.slot(ready).at[self.side] if self.split else self.slot(ready)
            self.finish(self.side, ready, slot, self.cross_slot(ready), self.result(ready, 0))
            self.back_copy(ready, 0).start()
            if self.split:
                self.share_copy(ready).start()

    def backs(self, tick):
        away = self.mid - 1 - self.hops
        unit0 = tick - self.start - self.mid - away

        @when_in(unit0, self.units, away > 0)
        def _():
            self.back_copy(unit0, 0).wait_recv()

        if self.mid > 2:

            @when_in(unit0, self.units, away > 0, self.hops > 0)
            def _():
                self.back_copy(unit0, 0).start()

        if self.split:
            unit1 = unit0 - 1

            @when_in(unit1, self.units)
            def _():
                self.back_copy(unit1, 1).wait_recv()

            @when_in(unit1, self.units, self.hops > 0)
            def _():
                self.back_copy(unit1, 1).start()

    def drain(self):
        @pl.loop(0, self.units)
        def _(unit):
            @pl.when(self.hops > 0)
            def _():
                self.back_copy(unit, 0).wait_send()
                if self.split:
                    self.back_copy(unit, 1).wait_send()

            if self.split:

                @pl.when(self.middle)
                def _():
                    self.share_copy(unit).wait_send()


class RowSum:
    def __init__(self, chips, units, start, buf, core_in, chip_in, sems, finish):
        self.chips, self.units, self.start = chips, units, start
        self.buf, self.core_in, self.chip_in = buf, core_in, chip_in
        self.finish = finish
        self.s1, self.r1, self.s2, self.r2 = sems
        self.done = start + 2
        row = lax.axis_index("row")
        self.core = lax.rem(row, 2)
        self.chip = lax.div(row, 2)
        self.partner = self.chip * 2 + 1 - self.core

    def first(self, unit):
        return pltpu.make_async_remote_copy(
            src_ref=self.buf.at[unit],
            dst_ref=self.core_in.at[lax.rem(unit, SLOTS)],
            send_sem=self.s1.at[unit],
            recv_sem=self.r1.at[unit],
            device_id={"row": self.partner},
            device_id_type=MESH,
        )

    def second(self, unit, step, core, arriving=False):
        half = core if arriving else self.core
        return pltpu.make_async_remote_copy(
            src_ref=self.buf.at[unit, half],
            dst_ref=self.chip_in.at[lax.rem(unit, SLOTS), step - 1, half],
            send_sem=self.s2.at[unit, step - 1, core],
            recv_sem=self.r2.at[unit, step - 1, half],
            device_id={"row": lax.rem(self.chip + step, self.chips) * 2 + core},
            device_id_type=MESH,
        )

    def begin(self, tick):
        unit = tick - self.start

        @when_in(unit, self.units)
        def _():
            self.first(unit).start()

    def steps(self, tick):
        others = [(step, core) for step in range(1, self.chips) for core in range(2)]
        unit2 = tick - self.start - 2

        @when_in(unit2, self.units)
        def _():
            for step, core in others:
                self.second(unit2, step, core, True).wait_recv()
            for step, core in others:
                self.second(unit2, step, core).wait_send()
            total = self.buf[unit2].astype(F32)
            for step in range(1, self.chips):
                total = total + self.chip_in[lax.rem(unit2, SLOTS), step - 1].astype(F32)
            self.buf[unit2] = self.finish(total)

        unit1 = tick - self.start - 1

        @when_in(unit1, self.units)
        def _():
            self.first(unit1).wait_recv()
            self.first(unit1).wait_send()
            self.buf[unit1] = (
                self.buf[unit1].astype(F32) + self.core_in[lax.rem(unit1, SLOTS)].astype(F32)
            ).astype(BF16)
            for step, core in others:
                self.second(unit1, step, core).start()


class Shares:
    def __init__(self, n, buf, sems):
        self.n, self.buf = n, buf
        self.send, self.recv = sems

    def copy(self, unit, step, arriving=False):
        me = lax.axis_index("col")
        slot = lax.rem(me + self.n - step, self.n) if arriving else me
        return pltpu.make_async_remote_copy(
            src_ref=self.buf.at[unit, slot],
            dst_ref=self.buf.at[unit, slot],
            send_sem=self.send.at[unit, step - 1],
            recv_sem=self.recv.at[unit, step - 1],
            device_id={"col": lax.rem(me + step, self.n)},
            device_id_type=MESH,
        )

    def put(self, unit, column):
        me = lax.axis_index("col")
        self.buf[unit, me] = jnp.broadcast_to(column, self.buf.shape[2:])
        for step in range(1, self.n):
            self.copy(unit, step).start()

    def wait(self, unit):
        for step in range(1, self.n):
            self.copy(unit, step, True).wait_recv()
            self.copy(unit, step).wait_send()

    def total(self, unit, rows=slice(None)):
        total = self.buf[unit, 0, rows]
        for index in range(1, self.n):
            total = total + self.buf[unit, index, rows]
        return total[:, :1]


def chain_kernel(
    n,
    chips,
    units,
    seq_ref,
    up_bias_ref,
    down_bias_ref,
    gain_ref,
    cot_ref,
    up_hbm,
    down_hbm,
    wg_hbm,
    wu_hbm,
    hidden_hbm,
    grad_merged_hbm,
    grad_pre_hbm,
    w_up_v,
    w_down_v,
    wg_v,
    wu_v,
    b_terms,
    b_in,
    b_cross,
    b_back,
    pre_act,
    c_buf,
    c_core,
    c_chip,
    squares,
    d_terms,
    d_in,
    d_cross,
    d_back,
    e_buf,
    e_core,
    e_chip,
    inners,
    f_terms,
    f_in,
    f_cross,
    f_back,
    w_sems,
    b_sems,
    d_sems,
    f_sems,
    credits,
    c_sem1,
    c_sem2,
    e_sem1,
    e_sem2,
    sq_sems,
    in_sems,
    out_sems,
):
    me = lax.axis_index("col")
    row = lax.axis_index("row")
    core = lax.rem(row, 2)
    chip = lax.div(row, 2)
    m = HALF
    rows = 2 * m

    loads = [
        pltpu.make_async_copy(src, dst, w_sems.at[k])
        for k, (src, dst) in enumerate(
            [(up_hbm, w_up_v), (down_hbm, w_down_v), (wg_hbm, wg_v), (wu_hbm, wu_v)]
        )
    ]
    for load in loads:
        load.start()

    barrier = pltpu.get_barrier_semaphore()
    for step in range(1, n):
        pl.semaphore_signal(
            barrier, inc=1, device_id={"col": lax.rem(me + step, n)}, device_id_type=MESH
        )
    pl.semaphore_signal(
        barrier, inc=1, device_id={"row": chip * 2 + 1 - core}, device_id_type=MESH
    )
    for step in range(1, chips):
        for to_core in range(2):
            pl.semaphore_signal(
                barrier,
                inc=1,
                device_id={"row": lax.rem(chip + step, chips) * 2 + to_core},
                device_id_type=MESH,
            )
    pl.semaphore_wait(barrier, n - 1 + 1 + 2 * (chips - 1))

    def gelu_finish(half, unit, ours, theirs, out):
        value = ours[:, 0].astype(F32) + theirs[:, 0].astype(F32) + up_bias_ref[...]
        pre_act[unit] = value
        out[:, 0] = (0.5 * value * (1.0 + lax.erf(value / math.sqrt(2.0)))).astype(BF16)

    def swiglu_finish(half, unit, ours, theirs, out):
        mine = pl.ds(pl.multiple_of(half * m, m), m)
        inv = lax.rsqrt(squares_io.total(unit, mine) / D + EPS_NORM)
        gate = ((ours[0].astype(F32) + theirs[0].astype(F32)) * inv).astype(BF16).astype(F32)
        up = ((ours[1].astype(F32) + theirs[1].astype(F32)) * inv).astype(BF16).astype(F32)
        masked = cot_ref[unit].astype(F32)
        logistic = 1.0 / (1.0 + jnp.exp(-gate))
        through = masked * logistic
        out[0] = (through * up * (1.0 + gate * (1.0 - logistic))).astype(BF16)
        out[1] = (through * gate).astype(BF16)

    def slope_finish(half, unit, ours, theirs, out):
        value = ours[:, 0].astype(F32) + theirs[:, 0].astype(F32)
        out[:, 0] = (value * gelu_slope(pre_act[unit])).astype(BF16)

    def parts(sems, count):
        return [sems.at[k] for k in range(count)]

    squares_io = Shares(n, squares, parts(sq_sems, 2))
    inners_io = Shares(n, inners, parts(in_sems, 2))
    line_b = Line(
        n,
        units,
        0,
        False,
        (b_terms, b_in, b_cross, b_back),
        parts(b_sems, 9),
        credits.at[0],
        gelu_finish,
    )
    sum_c = RowSum(
        chips,
        units,
        line_b.done,
        c_buf,
        c_core,
        c_chip,
        parts(c_sem1, 2) + parts(c_sem2, 2),
        lambda total: (total + down_bias_ref[...]).astype(BF16),
    )
    line_d = Line(
        n,
        units,
        sum_c.done + 2,
        True,
        (d_terms, d_in, d_cross, d_back),
        parts(d_sems, 9),
        credits.at[1],
        swiglu_finish,
    )
    sum_e = RowSum(
        chips,
        units,
        line_d.done + 2,
        e_buf,
        e_core,
        e_chip,
        parts(e_sem1, 2) + parts(e_sem2, 2),
        lambda total: total.astype(BF16),
    )
    line_f = Line(
        n,
        units,
        sum_e.done + 1,
        False,
        (f_terms, f_in, f_cross, f_back),
        parts(f_sems, 9),
        credits.at[2],
        slope_finish,
    )
    ticks = units + line_f.done + 1

    def out_copies(unit):
        return [
            pltpu.make_async_copy(src.at[unit], dst.at[unit], out_sems.at[k, unit])
            for k, (src, dst) in enumerate(
                [(b_back, hidden_hbm), (e_buf, grad_merged_hbm), (f_back, grad_pre_hbm)]
            )
        ]

    def tick_body(tick, carry):
        unit_q = tick - (sum_c.done + 1)

        @when_in(unit_q, units)
        def _():
            squares_io.wait(unit_q)

        line_d.sums(tick)
        line_d.backs(tick)

        unit_f = tick - line_f.start

        @when_in(unit_f, units)
        def _():
            inners_io.wait(unit_f)
            inv = lax.rsqrt(squares_io.total(unit_f) / D + EPS_NORM)
            factor = inv * inv * inv / D * inners_io.total(unit_f)
            merged = c_buf[unit_f].reshape(rows, -1).astype(F32)
            gained = e_buf[unit_f].reshape(rows, -1).astype(F32) * gain_ref[...]
            grad = (inv * gained - merged * factor).astype(BF16)
            e_buf[unit_f] = grad.reshape(2, m, -1)
            out_copies(unit_f)[1].start()
            slot = lax.rem(unit_f, f_terms.shape[0])
            for at, size in tiles_of(w_down_v.shape[0], 640):
                part = dot_cols(grad, w_down_v[pl.ds(at, size), :]).astype(BF16)
                f_terms[slot, :, 0, :, pl.ds(at, size)] = part.reshape(2, m, size)

        line_f.sums(tick)
        line_f.backs(tick)

        unit_z = tick - line_f.done

        @when_in(unit_z, units)
        def _():
            out_copies(unit_z)[2].start()

        sum_e.steps(tick)
        unit_i = tick - sum_e.done

        @when_in(unit_i, units)
        def _():
            merged = c_buf[unit_i].reshape(rows, -1).astype(F32)
            gained = e_buf[unit_i].reshape(rows, -1).astype(F32) * gain_ref[...]
            inners_io.put(unit_i, jnp.sum(merged * gained, axis=1, keepdims=True))

        sum_c.steps(tick)

        unit_s = tick - sum_c.done

        @when_in(unit_s, units)
        def _():
            merged = c_buf[unit_s].reshape(rows, -1).astype(F32)
            squares_io.put(unit_s, jnp.sum(merged * merged, axis=1, keepdims=True))

        @pl.when(tick == 0)
        def _():
            loads[0].wait()

        unit_b = tick

        @when_in(unit_b, units)
        def _():
            slot = lax.rem(unit_b, b_terms.shape[0])
            seq = seq_ref[unit_b].reshape(rows, -1)
            for at, size in tiles_of(w_up_v.shape[1], 640):
                part = dot_rows(seq, w_up_v[:, pl.ds(at, size)]).astype(BF16)
                b_terms[slot, :, 0, :, pl.ds(at, size)] = part.reshape(2, m, size)

        line_b.sums(tick)
        line_b.backs(tick)

        @pl.when(tick == sum_c.start)
        def _():
            loads[1].wait()

        unit_c = tick - sum_c.start

        @when_in(unit_c, units)
        def _():
            out_copies(unit_c)[0].start()
            hidden = b_back[unit_c, :, 0].reshape(rows, -1)
            for at, size in tiles_of(w_down_v.shape[1], 512):
                part = dot_rows(hidden, w_down_v[:, pl.ds(at, size)]).astype(BF16)
                c_buf[unit_c, :, :, pl.ds(at, size)] = part.reshape(2, m, size)

        sum_c.begin(tick)

        unit_e = tick - line_d.done - 2

        @when_in(unit_e, units, lax.rem(unit_e, 2) == 0)
        def _():
            pair = pl.ds(unit_e, 2)
            grad_gate = d_back[pair, :, 0].reshape(2 * rows, -1)
            grad_up = d_back[pair, :, 1].reshape(2 * rows, -1)
            for at, size in tiles_of(wg_v.shape[1], 512):
                part = (
                    dot_rows(grad_gate, wg_v[:, pl.ds(at, size)])
                    + dot_rows(grad_up, wu_v[:, pl.ds(at, size)])
                ).astype(BF16)
                e_buf[pair, :, :, pl.ds(at, size)] = part.reshape(2, 2, m, size)

        sum_e.begin(tick)

        @pl.when(tick == sum_c.done + 1)
        def _():
            loads[2].wait()
            loads[3].wait()

        unit_d = tick - sum_c.done - 1

        @when_in(unit_d, units, lax.rem(unit_d, 2) == 0)
        def _():
            merged = c_buf[pl.ds(unit_d, 2)].reshape(2 * rows, -1).astype(F32)
            lifted = (merged * gain_ref[...]).astype(BF16)
            slots = [lax.rem(unit_d + k, d_terms.shape[0]) for k in range(2)]
            for plane, weight in enumerate((wg_v, wu_v)):
                for at, size in tiles_of(weight.shape[0], 1024):
                    part = dot_cols(lifted, weight[pl.ds(at, size), :]).astype(BF16)
                    part = part.reshape(2, 2, m, size)
                    for k in range(2):
                        d_terms[slots[k], :, plane, :, pl.ds(at, size)] = part[k]

        return carry

    lax.fori_loop(0, ticks, tick_body, 0)
    line_b.drain()
    line_d.drain()
    line_f.drain()

    @pl.loop(0, units)
    def _(unit):
        for copy in out_copies(unit):
            copy.wait()


def chain(units, branch_id, seq, cot, operands):
    (
        merger_up,
        merger_up_bias,
        merger_down,
        merger_down_bias,
        norm_gain,
        w_gate,
        w_up,
    ) = operands
    n = lax.axis_size("col")
    chips = lax.axis_size("row") // 2
    m = HALF
    mdim, hid = merger_up.shape
    width = merger_down.shape[1]
    ffw = w_gate.shape[1]
    vmem = pl.BlockSpec(memory_space=pltpu.VMEM)
    hbm = pl.BlockSpec(memory_space=pltpu.HBM)
    dma = pltpu.SemaphoreType.DMA
    term_slots = max(SLOTS, n // 2 + 2)
    flops = 2 * units * 2 * m * (mdim * hid + 2 * hid * width + 4 * width * ffw)
    return pl.pallas_call(
        functools.partial(chain_kernel, n, chips, units),
        out_shape=[
            jax.ShapeDtypeStruct((units, 2, 1, m, hid), BF16),
            jax.ShapeDtypeStruct((units, 2, m, width), BF16),
            jax.ShapeDtypeStruct((units, 2, 1, m, hid), BF16),
        ],
        in_specs=[vmem] * 5 + [hbm] * 4,
        out_specs=[hbm] * 3,
        scratch_shapes=[
            pltpu.VMEM(merger_up.shape, BF16),
            pltpu.VMEM(merger_down.shape, BF16),
            pltpu.VMEM((ffw, width), BF16),
            pltpu.VMEM((ffw, width), BF16),
            pltpu.VMEM((term_slots, 2, 1, m, hid), BF16),
            pltpu.VMEM((SLOTS, 2, 1, m, hid), BF16),
            pltpu.VMEM((SLOTS, 2, 1, m, hid), BF16),
            pltpu.VMEM((units, 2, 1, m, hid), BF16),
            pltpu.VMEM((units, 2, m, hid), F32),
            pltpu.VMEM((units, 2, m, width), BF16),
            pltpu.VMEM((SLOTS, 2, m, width), BF16),
            pltpu.VMEM((SLOTS, chips - 1, 2, m, width), BF16),
            pltpu.VMEM((units, n, 2 * m, 128), F32),
            pltpu.VMEM((term_slots, 2, 2, m, ffw), BF16),
            pltpu.VMEM((SLOTS, 2, 2, m, ffw), BF16),
            pltpu.VMEM((SLOTS, 2, m, ffw), BF16),
            pltpu.VMEM((units, 2, 2, m, ffw), BF16),
            pltpu.VMEM((units, 2, m, width), BF16),
            pltpu.VMEM((SLOTS, 2, m, width), BF16),
            pltpu.VMEM((SLOTS, chips - 1, 2, m, width), BF16),
            pltpu.VMEM((units, n, 2 * m, 128), F32),
            pltpu.VMEM((term_slots, 2, 1, m, hid), BF16),
            pltpu.VMEM((SLOTS, 2, 1, m, hid), BF16),
            pltpu.VMEM((SLOTS, 2, 1, m, hid), BF16),
            pltpu.VMEM((units, 2, 1, m, hid), BF16),
            dma((4,)),
            dma((9, units)),
            dma((9, units)),
            dma((9, units)),
            pltpu.SemaphoreType.REGULAR((3,)),
            dma((2, units)),
            dma((2, units, chips - 1, 2)),
            dma((2, units)),
            dma((2, units, chips - 1, 2)),
            dma((2, units, n - 1)),
            dma((2, units, n - 1)),
            dma((3, units)),
        ],
        cost_estimate=pl.CostEstimate(
            flops=flops, bytes_accessed=2 * (mdim * hid + hid * width + 2 * width * ffw),
            transcendentals=units * m * ffw,
        ),
        compiler_params=pltpu.CompilerParams(
            collective_id=branch_id, has_side_effects=True, vmem_limit_bytes=63 * 1024 * 1024
        ),
    )(
        seq,
        merger_up_bias.astype(F32)[None],
        merger_down_bias.astype(F32)[None],
        norm_gain.astype(F32)[None],
        cot,
        merger_up,
        merger_down,
        w_gate.T,
        w_up.T,
    )


def half_plan(placement, patch_counts, tokens, n_col):
    images = placement.shape[0]
    ids = jnp.arange(images, dtype=jnp.int32)
    hit = placement[:, None] == ids[None, :]
    fill = jnp.sum(jnp.where(hit, (patch_counts // 4)[:, None], 0), axis=0)
    half = ids // (images // 2)
    before = (half[:, None] == half[None, :]) & (ids[None, :] < ids[:, None])
    start = jnp.sum(jnp.where(before, fill[None, :], 0), axis=1)
    place = jnp.arange(BLK, dtype=jnp.int32)
    rank = start[:, None] + place[None, :]
    real = place[None, :] < fill[:, None]
    slot = (rank // HALF) * (2 * HALF) + half[:, None] * HALF + rank % HALF
    slot = jnp.where(real, slot, -1)
    rank = jnp.where(real, rank, -1)
    by_image = jnp.sum(jnp.where(hit[:, :, None], slot[None, :, :], 0), axis=1)
    return rank.reshape(n_col, -1), by_image


def half_step(units, branch_id, sequence_in, cot_near, operands):
    (
        merger_up,
        merger_up_bias,
        merger_down,
        merger_down_bias,
        norm_gain,
        w_gate,
        w_up,
        hidden_cotangent,
        placement,
        patch_counts,
    ) = operands
    n_row = lax.axis_size("row")
    n_col = lax.axis_size("col")
    col_index = lax.axis_index("col")
    tokens = sequence_in.shape[0]
    rank, by_image = half_plan(placement, patch_counts, tokens, n_col)
    arrival = by_image.reshape(n_row, IMG_ROW, n_col, BLK // n_col)
    arrival = jnp.stack(
        [
            lax.dynamic_index_in_dim(arrival, (col_index - step) % n_col, axis=2, keepdims=False)
            for step in range(n_col)
        ],
        axis=1,
    ).reshape(-1)
    packed = units * 2 * HALF
    sequence = pick(one_hot(arrival, 0, packed), sequence_in).astype(BF16)
    near = n_col // 2
    rank_here = jnp.where(col_index >= near, rank[near:], rank[:near][::-1]).reshape(-1)
    cot = pick(one_hot(rank_here, 0, units * HALF), cot_near).astype(BF16)
    hidden_all, grad_merged_all, grad_pre_all = chain(
        units,
        branch_id,
        sequence.reshape(units, 2, HALF, -1),
        cot.reshape(units, HALF, -1),
        operands[:7],
    )
    hidden_all = hidden_all.reshape(packed, -1)
    grad_merged_all = grad_merged_all.reshape(packed, -1)
    grad_pre_all = grad_pre_all.reshape(packed, -1)
    merger_down_grad = lax.dot_general(
        hidden_all, grad_merged_all, CONTRACT_ROWS, preferred_element_type=F32
    )
    merger_down_bias_grad = jnp.sum(grad_merged_all, axis=0, dtype=F32)
    merger_up_grad = lax.dot_general(
        sequence, grad_pre_all, CONTRACT_ROWS, preferred_element_type=F32
    )
    merger_up_bias_grad = jnp.sum(grad_pre_all, axis=0, dtype=F32)
    return (merger_up_grad, merger_up_bias_grad, merger_down_grad, merger_down_bias_grad)


def shards(
    patches,
    patch_gain,
    patch_bias,
    merger_up,
    merger_up_bias,
    merger_down,
    merger_down_bias,
    norm_gain,
    w_gate,
    w_up,
    hidden_cotangent,
    placement,
    patch_counts,
):
    n_col = lax.axis_size("col")
    held = hidden_cotangent.shape[0]
    images = placement.shape[0]
    half_of = placement // (images // 2)
    in_half = jnp.where(
        half_of[:, None] == jnp.arange(2)[None, :], (patch_counts // 4)[:, None], 0
    )
    own_rows = jnp.max(jnp.sum(in_half, axis=0))
    real_rows = own_rows
    for step in range(1, lax.axis_size("group")):
        real_rows = jnp.maximum(real_rows, shift_by(own_rows, "group", step))
    most = held * n_col // 2 // HALF
    counts = [most * 5 // 8, most * 3 // 4]
    branch = sum((real_rows > units * HALF).astype(jnp.int32) for units in counts)
    near = [hidden_cotangent]
    for step in range(1, n_col // 2):
        near.append(
            lax.ppermute(
                hidden_cotangent,
                "col",
                [(n_col // 2 - 1 - step, n_col // 2 - 1), (n_col // 2 + step, n_col // 2)],
            )
        )
    cot_near = jnp.concatenate(near, axis=0)
    image_tokens = patch_tokens(patches, patch_gain, patch_bias)
    slot_count = image_tokens.shape[1]
    feat_width = image_tokens.shape[2] // n_col
    sending = image_tokens.reshape(IMG_ROW * slot_count, n_col, feat_width)
    sending = jnp.transpose(sending, (1, 0, 2))
    col_index = lax.axis_index("col")
    pieces = [lax.dynamic_index_in_dim(sending, col_index, keepdims=False)]
    for step in range(1, n_col):
        outgoing = lax.dynamic_index_in_dim(
            sending, (col_index + step) % n_col, keepdims=False
        )
        pieces.append(shift_by(outgoing, "col", step))
    merged = jnp.concatenate(pieces, axis=0)
    gathered_in = lax.all_gather(merged, "row", axis=0, tiled=True)
    operands = (
        merger_up,
        merger_up_bias,
        merger_down,
        merger_down_bias,
        norm_gain,
        w_gate,
        w_up,
        hidden_cotangent,
        placement,
        patch_counts,
    )
    steps = [
        functools.partial(half_step, units, number) for number, units in enumerate(counts)
    ]

    def whole_step(sequence_in, cot_near, operands):
        return packed_step(held, sequence_in, operands)

    return lax.switch(branch, steps + [whole_step], gathered_in, cot_near, operands)


def solution(mesh):
    in_specs = (
        P(("group", "row"), "col", None),
        P(),
        P(),
        P("col", "row"),
        P("row"),
        P("row", "col"),
        P("col"),
        P("col"),
        P("col", "row"),
        P("col", "row"),
        P(("group", "col"), "row"),
        P("group"),
        P("group"),
    )
    out_specs = (
        P(("group", "col"), "row"),
        P(("group", "row")),
        P(("group", "row"), "col"),
        P(("group", "col")),
    )
    return jax.shard_map(shards, mesh=mesh, in_specs=in_specs, out_specs=out_specs, check_vma=False)
```
